32 devices in a mesh: head: 8 (over z, y), dp: 4 (over x, core).
Axes of the slice: x: 2, y: 2, z: 4, core: 2. Of those that a mesh axis runs over, the one named last changes fastest.
Arguments:
- attn_out: bfloat16 [1024, 8192], P('dp', 'head'), may hold values from -6 to 6
- head_mask: int32 [64], P('head'), may hold values from 0 to 1, as said below
- gate_scale: float32 [64], P('head'), may hold values from 0.25 to 2
- w_out: bfloat16 [8192, 8192], P('head', 'dp'), may hold values from -0.09375 to 0.09375
- grad_out: bfloat16 [1024, 8192], P(('dp', 'head')), may hold values from -6 to 6
Outputs:
- proj_out: bfloat16 [1024, 8192], P(('dp', 'head'))
- grad_attn: bfloat16 [1024, 8192], P('dp', 'head')
- grad_w: float32 [8192, 8192], P('head', 'dp')
The draws below stay inside these ranges and needn't reach their ends.
Inputs may be any that keep to these rules, and one draw needn't show every extreme that they name: `head_mask`: exactly 32 heads are live.
All inputs are finite; a program needn't handle non-finite values.
Results may differ from the reference program's by a relative error of at most 0.0051.
Values may be sent and summed in bfloat16 or wider, within the bound.
A program may use at most 128 MiB of HBM per device.

```python
import math
import jax
import jax.numpy as jnp
from jax import lax

D = 8192
HEADS = 64
HEAD_DIM = 128
TOKENS = 1024


def draw_head_mask(key, part):
    order = jax.random.permutation(key, HEADS)
    return (order < HEADS // 2).astype(jnp.int32)


def block_levels(rng, extent, shards, low, largest):
    level, own = 1.0, jax.random.fold_in(rng, 6)
    for axis_at, shards_of in shards:
        steps = jnp.exp(jax.random.uniform(jax.random.fold_in(own, axis_at), (shards_of,), jnp.float32, low / len(shards), largest / len(shards)))
        level = level * jnp.repeat(steps, extent[axis_at] // shards_of).reshape([-1 if axis == axis_at else 1 for axis in range(len(extent))])
    return level


def gaussian(rng, extent, scale, most, split=(), dtype=jnp.bfloat16):
    entries = scale * jax.random.normal(rng, extent, jnp.float32)
    if split:
        entries = entries * block_levels(rng, extent, split, -0.22, 0.18)
    return jnp.clip(entries, -most, most).astype(dtype)


def setup_inputs(seed: int = 0) -> dict:
    keys = jax.random.split(jax.random.key(seed), 6)
    return {
        "attn_out": gaussian(keys[0], (TOKENS, HEADS * HEAD_DIM), 1.0, 6.0, ((0, 4), (1, 8))),
        "head_mask": draw_head_mask(jax.random.fold_in(keys[5], 71), 0),
        "gate_scale": jnp.clip(jnp.exp(math.log(2.0) - 2.0794415 * jax.random.uniform(keys[2], (HEADS,), jnp.float32) ** block_levels(keys[2], (HEADS,), ((0, 8),), -0.2, 0.2)), 0.25, 2.0),
        "w_out": gaussian(keys[3], (HEADS * HEAD_DIM, D), (HEADS * HEAD_DIM // 2) ** -0.5, 0.09375, ((0, 8), (1, 4))),
        "grad_out": gaussian(keys[4], (TOKENS, D), 1.0, 6.0, ((0, 32),)),
    }


def reference(attn_out, head_mask, gate_scale, w_out, grad_out):
    gate_vals = head_mask.astype(jnp.float32) * gate_scale
    col_gate = jnp.repeat(gate_vals, HEAD_DIM)
    gated = (attn_out.astype(jnp.float32) * col_gate[None, :]).astype(jnp.bfloat16)
    proj_out = jnp.dot(gated, w_out, preferred_element_type=jnp.float32).astype(jnp.bfloat16)
    back_proj = lax.dot_general(grad_out, w_out, (((1,), (1,)), ((), ())), preferred_element_type=jnp.float32)
    grad_attn = (back_proj * col_gate[None, :]).astype(jnp.bfloat16)
    grad_w = lax.dot_general(gated, grad_out, (((0,), (0,)), ((), ())), preferred_element_type=jnp.float32)
    return proj_out, grad_attn, grad_w
```

```python
import functools

import jax
import jax.numpy as jnp
from jax import lax
from jax.experimental import pallas as pl
from jax.experimental.pallas import tpu as pltpu
from jax.sharding import PartitionSpec as P

MESH = pl.DeviceIdType.MESH
F32, BF16 = jnp.float32, jnp.bfloat16
TILE = 256
SHARE = 5, 8
VMEM_LIMIT = 62 * 1024 * 1024


def split(cols):
    tiles = cols // TILE
    return max(1, min(tiles - 1, tiles * SHARE[0] // SHARE[1])) * TILE


def kernel(nh, nd, attn, mask, scale, grad, w_hbm, pj_hbm, ga_hbm, gt_hbm, g_hbm,
           gate, blocks, gated, gt, w, g, p0, p1, psy, ry, sz1, sz2, rz1, rz2, fb, ryf, fin, pj,
           bs, bo, br, bs2, br2, ga, ssem, rsem, lsem):
    na, nx = nh // 2, nd // 2
    h, d = lax.axis_index("head"), lax.axis_index("dp")
    z, b = h // 2, h % 2
    x, c = d // 2, d % 2
    rows, cols = g.shape[-2:]
    width = attn.shape[1]
    cut = split(cols)
    first, rest = pl.ds(0, cut), pl.ds(cut, cols - cut)
    sent = []
    ids = {}

    def when(cond, fn):
        if cond is None:
            fn()
        else:
            pl.when(cond)(fn)

    def slot(key):
        return ids.setdefault(key, len(ids))

    def remote(key, src, dst, dev):
        i = slot(key)
        return pltpu.make_async_remote_copy(
            src_ref=src, dst_ref=dst, send_sem=ssem.at[i], recv_sem=rsem.at[i],
            device_id=dev, device_id_type=MESH,
        )

    def send(key, cond, make, dev):
        when(cond, lambda: remote(key, *make(), dev).start())
        sent.append((key, cond, make, dev))

    def arrive(key, ref, dev):
        remote(key, ref, ref, dev).wait_recv()

    def dp(q):
        return {"head": h, "dp": q}

    def along(step):
        return {"head": (h + 2 * step + nh) % nh, "dp": d}

    beside = {"head": z * 2 + 1 - b, "dp": d}
    sibling = dp(x * 2 + 1 - c)

    def ahead(s):
        return ((x + s[0]) % nx) * 2 + (c + s[1]) % 2

    def behind(s):
        return ((x + nx - s[0]) % nx) * 2 + (c + s[1]) % 2

    far = [(kx, kc) for kx in range(1, nx) for kc in range(2)]

    def part(q):
        return grad.at[:, pl.ds(pl.multiple_of(q * cols, 128), cols)]

    w_copy = pltpu.make_async_copy(w_hbm, w, lsem.at[0])
    w_copy.start()
    own_copy = pltpu.make_async_copy(part(d), g.at[0, 0, z, 0], lsem.at[1])
    own_copy.start()

    heads = scale.shape[0]
    each = width // heads
    for i in range(heads):
        gate[:, i * each:(i + 1) * each] = jnp.full((1, each), mask[i].astype(F32) * scale[i], F32)

    barrier = pltpu.get_barrier_semaphore()

    def greet(dev):
        pl.semaphore_signal(barrier, inc=1, device_id=dev, device_id_type=MESH)

    for s in far + [(0, 1)]:
        greet(dp(ahead(s)))
    greet(beside)
    pl.when(z > 0)(lambda: greet(along(-1)))
    pl.when(z < na - 1)(lambda: greet(along(1)))
    pl.semaphore_wait(barrier, nd + (z + na - 1) // na + (2 * na - 2 - z) // na)

    for s in far + [(0, 1)]:
        send(("swap", s), None, lambda s=s: (part(ahead(s)), g.at[0, s[0], z, s[1]]), dp(ahead(s)))
    for k in range(1, nx):
        send(("attn", k), None, lambda k=k: (attn, blocks.at[k, 0]), dp(ahead((k, 0))))
    send(("attn", 0), None, lambda: (attn, blocks.at[0, 1]), sibling)

    def swapped(s):
        arrive(("swap", s), g.at[0, s[0], z, s[1]], dp(behind(s)))

    RIGHT, LEFT = 0, 1
    both = (RIGHT, LEFT)

    def unit(p, way):
        return z - p if way == RIGHT else z + p

    def held(p, way):
        return z >= p if way == RIGHT else z + p <= na - 1

    def open_to(way):
        return z < na - 1 if way == RIGHT else z > 0

    def open_from(way):
        return z > 0 if way == RIGHT else z < na - 1

    def step(way):
        return 1 if way == RIGHT else -1

    def ref_z(p, k, way, piece):
        u = unit(p, way)
        return g.at[0, k, u] if piece == 0 else g.at[1, k, u, :, :, rest]

    def gather_z(p, k, piece):
        for way in both:
            def make(way=way):
                ref = ref_z(p, k, way, piece)
                return ref, ref
            send(("gz", p, k, way, piece), held(p, way) & open_to(way), make, along(step(way)))

    def gathered_z(p, k, piece):
        for way in both:
            def wait(way=way):
                arrive(("gz", p - 1, k, way, piece), ref_z(p, k, way, piece), along(-step(way)))
            when(held(p, way), wait)

    def ref_y(p, k, way, r):
        return g.at[r, k, z] if p == 0 else g.at[r, k, unit(p, way), :, :, first]

    def gather_y(p, k):
        for way in both[:1] if p == 0 else both:
            def make(way=way):
                return ref_y(p, k, way, 0), ref_y(p, k, way, 1)
            send(("gy", p, k, way), None if p == 0 else held(p, way), make, beside)

    def gathered_y(p, k):
        for way in both[:1] if p == 0 else both:
            def wait(way=way):
                arrive(("gy", p, k, way), ref_y(p, k, way, 1), beside)
            when(None if p == 0 else held(p, way), wait)

    def due(p, way):
        return p > z if way == RIGHT else p > na - 1 - z

    def target(p, way):
        return na + z - p if way == RIGHT else z + p - na

    def sum_y(p, k):
        for way in both[:1] if p == na else both:
            def make(way=way):
                t = target(p, way)
                return psy.at[k, t], ry.at[k, t]
            send(("sy", p, k, way), None if p == na else due(p, way), make, beside)

    def tiles_of(lo, hi, fn):
        @pl.loop(lo // TILE, hi // TILE)
        def _(i):
            fn(pl.ds(pl.multiple_of(i * TILE, TILE), TILE), pl.ds(pl.multiple_of(i * TILE - cut, TILE), TILE))

    def sum_z(p, k):
        for way in both:
            def run(chained, way=way):
                t = target(p, way)
                arrive(("sy", p, k, way), ry.at[k, t], beside)
                if chained:
                    arrive(("sz", p - 1, k, way, 0), rz1.at[way, k, t], along(-step(way)))

                def front(at, _):
                    val = p0[k, t, :, :, at] + ry[k, t, :, :, at].astype(F32)
                    if chained:
                        val += rz1[way, k, t, :, :, at].astype(F32)
                    sz1[k, t, :, :, at] = val.astype(BF16)

                def back(at, _):
                    val = p0[k, t, :, :, at]
                    if chained:
                        val += rz1[way, k, t, :, :, at].astype(F32)
                    sz1[k, t, :, :, at] = val.astype(BF16)

                tiles_of(0, cut, front)
                tiles_of(cut, cols, back)

            def run2(chained, way=way):
                t = target(p, way)
                if chained:
                    arrive(("sz", p - 1, k, way, 1), rz2.at[way, k, t], along(-step(way)))

                def back(_, at):
                    val = p1[k, t, :, :, at]
                    if chained:
                        val += rz2[way, k, t, :, :, at].astype(F32)
                    sz2[k, t, :, :, at] = val.astype(BF16)

                tiles_of(cut, cols, back)

            now = due(p, way)
            for piece, fn, src, dst in ((0, run, sz1, rz1), (1, run2, sz2, rz2)):
                pl.when(now & open_from(way))(lambda fn=fn: fn(True))
                pl.when(now & jnp.logical_not(open_from(way)))(lambda fn=fn: fn(False))

                def make(way=way, src=src, dst=dst):
                    t = target(p, way)
                    return src.at[k, t], dst.at[way, k, t]
                send(("sz", p, k, way, piece), now, make, along(step(way)))

    def phase(p, k):
        gathered_z(p, k, 0)
        gather_z(p, k, 0)
        gather_y(p, k)
        sum_z(p, k)
        gathered_z(p, k, 1)
        gather_z(p, k, 1)
        sum_y(p + 1, k)

    def put(val, kx, kc):
        val = (val.astype(F32) * gate[...]).astype(BF16).reshape(na, 2, rows, width)
        for bb in range(2):
            gated[(b + bb) % 2, kx, :, kc] = val[:, bb]

    def turn(k):
        span = na * 2 * rows
        for r in range(2):
            lo = (r * nx + k) * span
            gt[:, lo:lo + span] = gated[r, k].reshape(span, width).T

    def project(k):
        def dot(at):
            lhs = gated[:, k].reshape(2 * na * 2 * rows, width)
            res = jnp.dot(lhs, w[:, at], preferred_element_type=F32)
            return res.reshape(2, na, 2, rows, TILE)

        def front(at, _):
            res = dot(at)
            p0[k, :, :, :, at] = res[0]
            psy[k, :, :, :, at] = res[1].astype(BF16)

        def back(at, low):
            res = dot(at)
            p0[k, :, :, :, at] = res[0]
            p1[k, :, :, :, low] = res[1]

        tiles_of(0, cut, front)
        tiles_of(cut, cols, back)

    small = jnp.minimum(z, na - 1 - z)

    def nth(j):
        if j == 0:
            return z
        near = z - (j + 1) // 2 if j % 2 else z + (j + 1) // 2
        end = jnp.where(z == small, j, na - 1 - j)
        return jnp.where(j <= 2 * small, near, end)

    def back(j):
        u = nth(j)
        if j:
            for k in range(nx):
                gathered_y(j, k)

        @pl.loop(0, width // TILE)
        def _(t):
            at = pl.ds(pl.multiple_of(t * TILE, TILE), TILE)
            lhs = g[:, :, u].reshape(2 * nx * 2 * rows, cols)
            res = lax.dot_general(lhs, w[at, :], (((1,), (1,)), ((), ())), preferred_element_type=F32)
            res = res.reshape(2, nx, 2, rows, TILE)
            bs[j, :, :, :, at] = res[:, :, 1].astype(BF16)
            bo[j, :, :, :, at] = res[:, :, 0]

        send(("pair", j), None, lambda: (bs.at[j], br.at[j]), sibling)

    def cross(j):
        arrive(("pair", j), br.at[j], sibling)
        for k in range(1, nx):
            bs2[j, k - 1] = (bo[j, :, k] + br[j, :, k].astype(F32)).astype(BF16)
            send(("cross", j, k), None, lambda k=k: (bs2.at[j, k - 1], br2.at[j, k - 1]), dp(behind((k, 0))))

    own_copy.wait()
    swapped((0, 1))
    gather_z(0, 0, 0)
    gather_y(0, 0)
    put(attn[...], 0, 0)
    arrive(("attn", 0), blocks.at[0, 1], sibling)
    put(blocks[0, 1], 0, 1)
    w_copy.wait()
    project(0)
    for k in range(1, nx):
        for kc in range(2):
            swapped((k, kc))
        gather_z(0, k, 0)
        gather_y(0, k)
    gathered_y(0, 0)
    gather_z(0, 0, 1)
    sum_y(1, 0)
    phase(1, 0)
    turn(0)
    for k in range(1, nx):
        gathered_y(0, k)
        gather_z(0, k, 1)
    for k in range(1, nx):
        arrive(("attn", k), blocks.at[k, 0], dp(behind((k, 0))))
        send(("pass", k), None, lambda k=k: (blocks.at[k, 0], blocks.at[k, 1]), sibling)
        put(blocks[k, 0], k, 0)
    for k in range(1, nx):
        arrive(("pass", k), blocks.at[k, 1], sibling)
        put(blocks[k, 1], k, 1)
        project(k)
        sum_y(1, k)
        phase(1, k)
        turn(k)
    gt_copy = pltpu.make_async_copy(gt, gt_hbm, lsem.at[2])
    gt_copy.start()

    back(0)
    for p in range(2, na):
        for k in range(nx):
            phase(p, k)
        cross(p - 2)
        back(p - 1)
    cross(na - 2)
    back(na - 1)
    g_copy = pltpu.make_async_copy(g, g_hbm, lsem.at[3])
    g_copy.start()

    def add_in(dst, lo, piece, k, way, buf):
        def run():
            arrive(("sz", na - 1, k, way, piece), buf.at[way, k, z], along(-step(way)))

            def tile(at, low):
                at = low if piece else at
                dst[k, z, :, :, at] += buf[way, k, z, :, :, at].astype(F32)
            tiles_of(lo, cols, tile)
        pl.when(open_from(way))(run)

    for k in range(nx):
        for way in both:
            add_in(p1, cut, 1, k, way, rz2)
        fb[k] = p1[k, z].astype(BF16)
        send(("fy", k), None, lambda k=k: (fb.at[k], ryf.at[k]), beside)
    for k in range(nx):
        for way in both:
            add_in(p0, 0, 0, k, way, rz1)
    cross(na - 1)

    def finish(k):
        arrive(("sy", na, k, RIGHT), ry.at[k, z], beside)

        def front(at, _):
            fin[k, :, :, at] = (p0[k, z, :, :, at] + ry[k, z, :, :, at].astype(F32)).astype(BF16)

        tiles_of(0, cut, front)
        arrive(("fy", k), ryf.at[k], beside)

        def rear(at, low):
            fin[k, :, :, at] = (p0[k, z, :, :, at] + ryf[k, :, :, low].astype(F32)).astype(BF16)

        tiles_of(cut, cols, rear)
        for kc in range(2):
            if (k, kc) != (0, 0):
                send(("home", (k, kc)), None, lambda kc=kc: (fin.at[k, kc], pj.at[d]), dp(behind((k, kc))))

    for k in list(range(1, nx)) + [0]:
        finish(k)
    pj[d] = fin[0, 0]

    for j in range(na):
        for k in range(1, nx):
            arrive(("cross", j, k), br2.at[j, k - 1], dp(ahead((k, 0))))
        total = bo[j, :, 0] + br[j, :, 0].astype(F32)
        for k in range(1, nx):
            total += br2[j, k - 1].astype(F32)
        total = (total * gate[...].reshape(1, 1, width)).astype(BF16)
        for r in range(2):
            ga[nth(j), (b + r) % 2] = total[r]
    ga_copy = pltpu.make_async_copy(ga, ga_hbm, lsem.at[4])
    ga_copy.start()
    for s in [(0, 1)] + far:
        arrive(("home", s), pj.at[ahead(s)], dp(ahead(s)))
    pj_copy = pltpu.make_async_copy(pj, pj_hbm, lsem.at[5])
    pj_copy.start()
    for key, cond, make, dev in sent:
        when(cond, lambda: remote(key, *make(), dev).wait_send())
    gt_copy.wait()
    g_copy.wait()
    ga_copy.wait()
    pj_copy.wait()


def weight_kernel(gt, g, pj, ga, gw, proj, gattn):
    width = gt.shape[0]

    @pl.loop(0, width // TILE)
    def _(t):
        at = pl.ds(pl.multiple_of(t * TILE, TILE), TILE)
        gw[at, :] = jnp.dot(gt[at, :], g[...], preferred_element_type=F32)

    proj[...] = pj[0]
    gattn[...] = ga[...]


def fused(nh, nd, attn_out, head_mask, gate_scale, w_out, grad_out):
    na, nx = nh // 2, nd // 2
    rows, cols, width = grad_out.shape[0], w_out.shape[1], w_out.shape[0]
    tokens = rows * nh * nd
    cut = split(cols)
    n_sems = 2 * nd + 4 * nx + 11 * (na + 1) * nx * 2 + na * nx
    vmem = pl.BlockSpec(memory_space=pltpu.VMEM)
    smem = pl.BlockSpec(memory_space=pltpu.SMEM)
    hbm = pl.BlockSpec(memory_space=pl.ANY)
    order = (2, nx, na, 2, rows)
    half = (nx, na, 2, rows)
    pj, ga, gt, g = pl.pallas_call(
        functools.partial(kernel, nh, nd),
        out_shape=(
            jax.ShapeDtypeStruct((nd, rows, cols), BF16),
            jax.ShapeDtypeStruct((na, 2, rows, width), BF16),
            jax.ShapeDtypeStruct((width, tokens), BF16),
            jax.ShapeDtypeStruct(order + (cols,), BF16),
        ),
        in_specs=[vmem, smem, smem, vmem, hbm],
        out_specs=(hbm, hbm, hbm, hbm),
        scratch_shapes=[
            pltpu.VMEM((1, width), F32),
            pltpu.VMEM((nx, 2, nh * rows, width), BF16),
            pltpu.VMEM(order + (width,), BF16),
            pltpu.VMEM((width, tokens), BF16),
            pltpu.VMEM(w_out.shape, BF16),
            pltpu.VMEM(order + (cols,), BF16),
            pltpu.VMEM(half + (cols,), F32),
            pltpu.VMEM(half + (cols - cut,), F32),
            pltpu.VMEM(half + (cut,), BF16),
            pltpu.VMEM(half + (cut,), BF16),
            pltpu.VMEM(half + (cols,), BF16),
            pltpu.VMEM(half + (cols - cut,), BF16),
            pltpu.VMEM((2,) + half + (cols,), BF16),
            pltpu.VMEM((2,) + half + (cols - cut,), BF16),
            pltpu.VMEM((nx, 2, rows, cols - cut), BF16),
            pltpu.VMEM((nx, 2, rows, cols - cut), BF16),
            pltpu.VMEM((nx, 2, rows, cols), BF16),
            pltpu.VMEM((nd, rows, cols), BF16),
            pltpu.VMEM((na, 2, nx, rows, width), BF16),
            pltpu.VMEM((na, 2, nx, rows, width), F32),
            pltpu.VMEM((na, 2, nx, rows, width), BF16),
            pltpu.VMEM((na, nx - 1, 2, rows, width), BF16),
            pltpu.VMEM((na, nx - 1, 2, rows, width), BF16),
            pltpu.VMEM((na, 2, rows, width), BF16),
            pltpu.SemaphoreType.DMA((n_sems,)),
            pltpu.SemaphoreType.DMA((n_sems,)),
            pltpu.SemaphoreType.DMA((6,)),
        ],
        compiler_params=pltpu.CompilerParams(
            collective_id=0, has_side_effects=True, vmem_limit_bytes=VMEM_LIMIT
        ),
    )(attn_out, head_mask, gate_scale, grad_out, w_out)
    each = tokens // nd // nd
    gw, proj, gattn = pl.pallas_call(
        weight_kernel,
        grid=(nd,),
        out_shape=(
            jax.ShapeDtypeStruct(w_out.shape, F32),
            jax.ShapeDtypeStruct(grad_out.shape, BF16),
            jax.ShapeDtypeStruct(attn_out.shape, BF16),
        ),
        in_specs=[
            pl.BlockSpec((width, tokens), lambda i: (0, 0)),
            pl.BlockSpec((tokens, cols // nd), lambda i: (0, i)),
            pl.BlockSpec((1, rows, cols), lambda i: (i, 0, 0)),
            pl.BlockSpec((each, width), lambda i: (i, 0)),
        ],
        out_specs=(
            pl.BlockSpec((width, cols // nd), lambda i: (0, i)),
            pl.BlockSpec((rows, cols), lambda i: (0, i)),
            pl.BlockSpec((each, width), lambda i: (i, 0)),
        ),
        compiler_params=pltpu.CompilerParams(vmem_limit_bytes=VMEM_LIMIT // 2),
    )(gt, g.reshape(tokens, cols), pj, ga.reshape(attn_out.shape))
    return proj, gattn, gw


def shards(attn_out, head_mask, gate_scale, w_out, grad_out):
    n_dp, n_head = lax.axis_size("dp"), lax.axis_size("head")
    rows, (width, cols) = grad_out.shape[0], w_out.shape
    if rows % 16 == 0 and n_dp % 2 == 0 and n_head % 2 == 0 and min(n_dp, n_head) > 2 and width % TILE == 0 and cols % (2 * TILE) == 0 and cols % (n_dp * 128) == 0 and (width // head_mask.shape[0]) % 128 == 0 and n_head * rows % n_dp == 0:
        return fused(n_head, n_dp, attn_out, head_mask, gate_scale, w_out, grad_out)
    gate_vals = head_mask.astype(jnp.float32) * gate_scale
    width_each = attn_out.shape[1] // gate_vals.shape[0]
    col_gate = jnp.repeat(gate_vals, width_each)
    gated = (attn_out.astype(jnp.float32) * col_gate[None, :]).astype(jnp.bfloat16)
    mine = lax.all_to_all(grad_out, "dp", 1, 0, tiled=True)
    every = lax.all_gather(mine.reshape(n_dp, rows, cols), "head", axis=1)
    grad_cols = every.reshape(n_dp * n_head * rows, cols)
    gated_all = lax.all_gather(gated, "dp", axis=0, tiled=True)
    part = jnp.dot(gated_all, w_out, preferred_element_type=jnp.float32).astype(jnp.bfloat16)
    summed = lax.psum_scatter(part.reshape(n_dp, n_head, rows, cols), "head", scatter_dimension=1, tiled=False)
    proj_out = lax.all_to_all(summed.reshape(n_dp * rows, cols), "dp", 0, 1, tiled=True)
    back = lax.dot_general(grad_cols, w_out, (((1,), (1,)), ((), ())), preferred_element_type=jnp.float32)
    back = lax.psum_scatter(back.astype(jnp.bfloat16), "dp", scatter_dimension=0, tiled=True)
    grad_attn = (back.astype(jnp.float32) * col_gate[None, :]).astype(jnp.bfloat16)
    grad_w = lax.dot_general(gated_all, grad_cols, (((0,), (0,)), ((), ())), preferred_element_type=jnp.float32)
    return (proj_out, grad_attn, grad_w)


def solution(mesh):
    return jax.shard_map(
        shards,
        mesh=mesh,
        in_specs=(P("dp", "head"), P("head"), P("head"), P("head", "dp"), P(("dp", "head"), None)),
        out_specs=(P(("dp", "head"), None), P("dp", "head"), P("head", "dp")),
        check_vma=False,
    )
```

```python
import functools

import jax
import jax.numpy as jnp
from jax import lax
from jax.experimental import pallas as pl
from jax.experimental.pallas import tpu as pltpu
from jax.sharding import PartitionSpec as P

MESH = pl.DeviceIdType.MESH
F32, BF16 = jnp.float32, jnp.bfloat16
TILE = 256
SHARE = 5, 8
VMEM_LIMIT = 44 * 1024 * 1024
WEIGHT_LIMIT = 16 * 1024 * 1024


def split(cols):
    tiles = cols // TILE
    return max(1, min(tiles - 1, tiles * SHARE[0] // SHARE[1])) * TILE


def kernel(nh, nd, attn, mask_hbm, scale_hbm, grad, w_hbm, pj_hbm, ga_hbm, gt_hbm, g_hbm,
           mask, scale, gate, blocks, gated, gt, w, g, p0, p1, psy, ry, sz1, sz2, rz1, rz2, fb, ryf, fin, pj,
           bs, bo, br, bs2, br2, ga, ssem, rsem, lsem):
    na, nx = nh // 2, nd // 2
    h, d = lax.axis_index("head"), lax.axis_index("dp")
    z, b = h // 2, h % 2
    x, c = d // 2, d % 2
    rows, cols = g.shape[-2:]
    width = attn.shape[1]
    cut = split(cols)
    first, rest = pl.ds(0, cut), pl.ds(cut, cols - cut)
    sent = []
    ids = {}

    def when(cond, fn):
        if cond is None:
            fn()
        else:
            pl.when(cond)(fn)

    def slot(key):
        return ids.setdefault(key, len(ids))

    def remote(key, src, dst, dev):
        i = slot(key)
        return pltpu.make_async_remote_copy(
            src_ref=src, dst_ref=dst, send_sem=ssem.at[i], recv_sem=rsem.at[i],
            device_id=dev, device_id_type=MESH,
        )

    def send(key, cond, make, dev):
        when(cond, lambda: remote(key, *make(), dev).start())
        sent.append((key, cond, make, dev))

    def arrive(key, ref, dev):
        remote(key, ref, ref, dev).wait_recv()

    def dp(q):
        return {"head": h, "dp": q}

    def along(step):
        return {"head": (h + 2 * step + nh) % nh, "dp": d}

    beside = {"head": z * 2 + 1 - b, "dp": d}
    sibling = dp(x * 2 + 1 - c)

    def ahead(s):
        return ((x + s[0]) % nx) * 2 + (c + s[1]) % 2

    def behind(s):
        return ((x + nx - s[0]) % nx) * 2 + (c + s[1]) % 2

    far = [(kx, kc) for kx in range(1, nx) for kc in range(2)]

    def part(q):
        return grad.at[:, pl.ds(pl.multiple_of(q * cols, 128), cols)]

    w_copy = pltpu.make_async_copy(w_hbm, w, lsem.at[0])
    w_copy.start()
    own_copy = pltpu.make_async_copy(part(d), g.at[0, 0, z, 0], lsem.at[1])
    own_copy.start()
    mask_copy = pltpu.make_async_copy(mask_hbm, mask, lsem.at[6])
    mask_copy.start()
    scale_copy = pltpu.make_async_copy(scale_hbm, scale, lsem.at[7])
    scale_copy.start()
    attn_copy = pltpu.make_async_copy(attn, blocks.at[0, 0], lsem.at[8])
    attn_copy.start()

    barrier = pltpu.get_barrier_semaphore()

    def greet(dev):
        pl.semaphore_signal(barrier, inc=1, device_id=dev, device_id_type=MESH)

    for s in far + [(0, 1)]:
        greet(dp(ahead(s)))
    greet(beside)
    pl.when(z > 0)(lambda: greet(along(-1)))
    pl.when(z < na - 1)(lambda: greet(along(1)))
    pl.semaphore_wait(barrier, nd + (z + na - 1) // na + (2 * na - 2 - z) // na)

    for s in far + [(0, 1)]:
        send(("swap", s), None, lambda s=s: (part(ahead(s)), g.at[0, s[0], z, s[1]]), dp(ahead(s)))
    for k in range(1, nx):
        send(("attn", k), None, lambda k=k: (attn, blocks.at[k, 0]), dp(ahead((k, 0))))
    send(("attn", 0), None, lambda: (attn, blocks.at[0, 1]), sibling)

    def swapped(s):
        arrive(("swap", s), g.at[0, s[0], z, s[1]], dp(behind(s)))

    RIGHT, LEFT = 0, 1
    both = (RIGHT, LEFT)

    def unit(p, way):
        return z - p if way == RIGHT else z + p

    def held(p, way):
        return z >= p if way == RIGHT else z + p <= na - 1

    def open_to(way):
        return z < na - 1 if way == RIGHT else z > 0

    def open_from(way):
        return z > 0 if way == RIGHT else z < na - 1

    def step(way):
        return 1 if way == RIGHT else -1

    def ref_z(p, k, way, piece):
        u = unit(p, way)
        return g.at[0, k, u] if piece == 0 else g.at[1, k, u, :, :, rest]

    def gather_z(p, k, piece):
        for way in both:
            def make(way=way):
                ref = ref_z(p, k, way, piece)
                return ref, ref
            send(("gz", p, k, way, piece), held(p, way) & open_to(way), make, along(step(way)))

    def gathered_z(p, k, piece):
        for way in both:
            def wait(way=way):
                arrive(("gz", p - 1, k, way, piece), ref_z(p, k, way, piece), along(-step(way)))
            when(held(p, way), wait)

    def ref_y(p, k, way, r):
        return g.at[r, k, z] if p == 0 else g.at[r, k, unit(p, way), :, :, first]

    def gather_y(p, k):
        for way in both[:1] if p == 0 else both:
            def make(way=way):
                return ref_y(p, k, way, 0), ref_y(p, k, way, 1)
            send(("gy", p, k, way), None if p == 0 else held(p, way), make, beside)

    def gathered_y(p, k):
        for way in both[:1] if p == 0 else both:
            def wait(way=way):
                arrive(("gy", p, k, way), ref_y(p, k, way, 1), beside)
            when(None if p == 0 else held(p, way), wait)

    def due(p, way):
        return p > z if way == RIGHT else p > na - 1 - z

    def target(p, way):
        return na + z - p if way == RIGHT else z + p - na

    def sum_y(p, k):
        for way in both[:1] if p == na else both:
            def make(way=way):
                t = target(p, way)
                return psy.at[k, t], ry.at[k, t]
            send(("sy", p, k, way), None if p == na else due(p, way), make, beside)

    def tiles_of(lo, hi, fn):
        @pl.loop(lo // TILE, hi // TILE)
        def _(i):
            fn(pl.ds(pl.multiple_of(i * TILE, TILE), TILE), pl.ds(pl.multiple_of(i * TILE - cut, TILE), TILE))

    def sum_z(p, k):
        for way in both:
            def run(chained, way=way):
                t = target(p, way)
                arrive(("sy", p, k, way), ry.at[k, t], beside)
                if chained:
                    arrive(("sz", p - 1, k, way, 0), rz1.at[way, k, t], along(-step(way)))

                def front(at, _):
                    val = p0[k, t, :, :, at] + ry[k, t, :, :, at].astype(F32)
                    if chained:
                        val += rz1[way, k, t, :, :, at].astype(F32)
                    sz1[k, t, :, :, at] = val.astype(BF16)

                def back(at, _):
                    val = p0[k, t, :, :, at]
                    if chained:
                        val += rz1[way, k, t, :, :, at].astype(F32)
                    sz1[k, t, :, :, at] = val.astype(BF16)

                tiles_of(0, cut, front)
                tiles_of(cut, cols, back)

            def run2(chained, way=way):
                t = target(p, way)
                if chained:
                    arrive(("sz", p - 1, k, way, 1), rz2.at[way, k, t], along(-step(way)))

                def back(_, at):
                    val = p1[k, t, :, :, at]
                    if chained:
                        val += rz2[way, k, t, :, :, at].astype(F32)
                    sz2[k, t, :, :, at] = val.astype(BF16)

                tiles_of(cut, cols, back)

            now = due(p, way)
            for piece, fn, src, dst in ((0, run, sz1, rz1), (1, run2, sz2, rz2)):
                pl.when(now & open_from(way))(lambda fn=fn: fn(True))
                pl.when(now & jnp.logical_not(open_from(way)))(lambda fn=fn: fn(False))

                def make(way=way, src=src, dst=dst):
                    t = target(p, way)
                    return src.at[k, t], dst.at[way, k, t]
                send(("sz", p, k, way, piece), now, make, along(step(way)))

    def phase(p, k):
        gathered_z(p, k, 0)
        gather_z(p, k, 0)
        gather_y(p, k)
        sum_z(p, k)
        gathered_z(p, k, 1)
        gather_z(p, k, 1)
        sum_y(p + 1, k)

    def put(val, kx, kc):
        val = (val.astype(F32) * gate[...]).astype(BF16).reshape(na, 2, rows, width)
        for bb in range(2):
            gated[(b + bb) % 2, kx, :, kc] = val[:, bb]

    def turn(k):
        span = na * 2 * rows
        for r in range(2):
            lo = (r * nx + k) * span
            gt[:, lo:lo + span] = gated[r, k].reshape(span, width).T

    def project(k):
        def dot(at):
            lhs = gated[:, k].reshape(2 * na * 2 * rows, width)
            res = jnp.dot(lhs, w[:, at], preferred_element_type=F32)
            return res.reshape(2, na, 2, rows, TILE)

        def front(at, _):
            res = dot(at)
            p0[k, :, :, :, at] = res[0]
            psy[k, :, :, :, at] = res[1].astype(BF16)

        def back(at, low):
            res = dot(at)
            p0[k, :, :, :, at] = res[0]
            p1[k, :, :, :, low] = res[1]

        tiles_of(0, cut, front)
        tiles_of(cut, cols, back)

    small = jnp.minimum(z, na - 1 - z)

    def nth(j):
        if j == 0:
            return z
        near = z - (j + 1) // 2 if j % 2 else z + (j + 1) // 2
        end = jnp.where(z == small, j, na - 1 - j)
        return jnp.where(j <= 2 * small, near, end)

    def back(j):
        u = nth(j)
        if j:
            for k in range(nx):
                gathered_y(j, k)

        @pl.loop(0, width // TILE)
        def _(t):
            at = pl.ds(pl.multiple_of(t * TILE, TILE), TILE)
            lhs = g[:, :, u].reshape(2 * nx * 2 * rows, cols)
            res = lax.dot_general(lhs, w[at, :], (((1,), (1,)), ((), ())), preferred_element_type=F32)
            res = res.reshape(2, nx, 2, rows, TILE)
            bs[j, :, :, :, at] = res[:, :, 1].astype(BF16)
            bo[j, :, :, :, at] = res[:, :, 0]

        send(("pair", j), None, lambda: (bs.at[j], br.at[j]), sibling)

    def cross(j):
        arrive(("pair", j), br.at[j], sibling)
        for k in range(1, nx):
            bs2[j, k - 1] = (bo[j, :, k] + br[j, :, k].astype(F32)).astype(BF16)
            send(("cross", j, k), None, lambda k=k: (bs2.at[j, k - 1], br2.at[j, k - 1]), dp(behind((k, 0))))

    own_copy.wait()
    swapped((0, 1))
    gather_z(0, 0, 0)
    gather_y(0, 0)
    mask_copy.wait()
    scale_copy.wait()
    heads = scale.shape[0]
    each = width // heads
    for i in range(heads):
        gate[:, i * each:(i + 1) * each] = jnp.full((1, each), mask[i].astype(F32) * scale[i], F32)
    attn_copy.wait()
    put(blocks[0, 0], 0, 0)
    arrive(("attn", 0), blocks.at[0, 1], sibling)
    put(blocks[0, 1], 0, 1)
    w_copy.wait()
    project(0)
    for k in range(1, nx):
        for kc in range(2):
            swapped((k, kc))
        gather_z(0, k, 0)
        gather_y(0, k)
    gathered_y(0, 0)
    gather_z(0, 0, 1)
    sum_y(1, 0)
    phase(1, 0)
    turn(0)
    for k in range(1, nx):
        gathered_y(0, k)
        gather_z(0, k, 1)
    for k in range(1, nx):
        arrive(("attn", k), blocks.at[k, 0], dp(behind((k, 0))))
        send(("pass", k), None, lambda k=k: (blocks.at[k, 0], blocks.at[k, 1]), sibling)
        put(blocks[k, 0], k, 0)
    for k in range(1, nx):
        arrive(("pass", k), blocks.at[k, 1], sibling)
        put(blocks[k, 1], k, 1)
        project(k)
        sum_y(1, k)
        phase(1, k)
        turn(k)
    gt_copy = pltpu.make_async_copy(gt, gt_hbm, lsem.at[2])
    gt_copy.start()

    back(0)
    for p in range(2, na):
        for k in range(nx):
            phase(p, k)
        cross(p - 2)
        back(p - 1)
    cross(na - 2)
    back(na - 1)
    g_copy = pltpu.make_async_copy(g, g_hbm, lsem.at[3])
    g_copy.start()

    def add_in(dst, lo, piece, k, way, buf):
        def run():
            arrive(("sz", na - 1, k, way, piece), buf.at[way, k, z], along(-step(way)))

            def tile(at, low):
                at = low if piece else at
                dst[k, z, :, :, at] += buf[way, k, z, :, :, at].astype(F32)
            tiles_of(lo, cols, tile)
        pl.when(open_from(way))(run)

    for k in range(nx):
        for way in both:
            add_in(p1, cut, 1, k, way, rz2)
        fb[k] = p1[k, z].astype(BF16)
        send(("fy", k), None, lambda k=k: (fb.at[k], ryf.at[k]), beside)
    for k in range(nx):
        for way in both:
            add_in(p0, 0, 0, k, way, rz1)
    cross(na - 1)

    def finish(k):
        arrive(("sy", na, k, RIGHT), ry.at[k, z], beside)

        def front(at, _):
            fin[k, :, :, at] = (p0[k, z, :, :, at] + ry[k, z, :, :, at].astype(F32)).astype(BF16)

        tiles_of(0, cut, front)
        arrive(("fy", k), ryf.at[k], beside)

        def rear(at, low):
            fin[k, :, :, at] = (p0[k, z, :, :, at] + ryf[k, :, :, low].astype(F32)).astype(BF16)

        tiles_of(cut, cols, rear)
        for kc in range(2):
            if (k, kc) != (0, 0):
                send(("home", (k, kc)), None, lambda kc=kc: (fin.at[k, kc], pj.at[d]), dp(behind((k, kc))))

    for k in list(range(1, nx)) + [0]:
        finish(k)
    pj[d] = fin[0, 0]

    for j in range(na):
        for k in range(1, nx):
            arrive(("cross", j, k), br2.at[j, k - 1], dp(ahead((k, 0))))
        total = bo[j, :, 0] + br[j, :, 0].astype(F32)
        for k in range(1, nx):
            total += br2[j, k - 1].astype(F32)
        total = (total * gate[...].reshape(1, 1, width)).astype(BF16)
        for r in range(2):
            ga[nth(j), (b + r) % 2] = total[r]
    ga_copy = pltpu.make_async_copy(ga, ga_hbm, lsem.at[4])
    ga_copy.start()
    for s in [(0, 1)] + far:
        arrive(("home", s), pj.at[ahead(s)], dp(ahead(s)))
    pj_copy = pltpu.make_async_copy(pj, pj_hbm, lsem.at[5])
    pj_copy.start()
    for key, cond, make, dev in sent:
        when(cond, lambda: remote(key, *make(), dev).wait_send())
    gt_copy.wait()
    g_copy.wait()
    ga_copy.wait()
    pj_copy.wait()


def weight_kernel(gt, g, pj, ga, gw, proj, gattn, stage, osem, psem):
    cols = g.shape[1]
    span = stage.shape[2]
    others = [pltpu.make_async_copy(ga, gattn, psem.at[0])]
    for i in range(pj.shape[0]):
        others.append(pltpu.make_async_copy(pj.at[i], proj.at[:, i * cols:(i + 1) * cols], psem.at[i + 1]))
    for copy in others:
        copy.start()
    out = []
    for i in range(cols // span):
        slot, at = i % 2, slice(i * span, (i + 1) * span)
        if i >= 2:
            out[i - 2].wait()
        stage[slot] = jnp.dot(gt[...], g[:, at], preferred_element_type=F32)
        out.append(pltpu.make_async_copy(stage.at[slot], gw.at[:, at], osem.at[slot]))
        out[i].start()
    for copy in out[-2:] + others:
        copy.wait()


def fused(nh, nd, attn_out, head_mask, gate_scale, w_out, grad_out):
    na, nx = nh // 2, nd // 2
    rows, cols, width = grad_out.shape[0], w_out.shape[1], w_out.shape[0]
    tokens = rows * nh * nd
    cut = split(cols)
    n_sems = 2 * nd + 4 * nx + 11 * (na + 1) * nx * 2 + na * nx
    vmem = pl.BlockSpec(memory_space=pltpu.VMEM)
    hbm = pl.BlockSpec(memory_space=pltpu.HBM)
    free = pl.BlockSpec(memory_space=pl.ANY)
    order = (2, nx, na, 2, rows)
    half = (nx, na, 2, rows)
    pj, ga, gt, g = pl.pallas_call(
        functools.partial(kernel, nh, nd),
        out_shape=(
            jax.ShapeDtypeStruct((nd, rows, cols), BF16),
            jax.ShapeDtypeStruct((na, 2, rows, width), BF16),
            jax.ShapeDtypeStruct((width, tokens), BF16),
            jax.ShapeDtypeStruct(order + (cols,), BF16),
        ),
        in_specs=[hbm] * 5,
        out_specs=(free,) * 4,
        scratch_shapes=[
            pltpu.SMEM(head_mask.shape, head_mask.dtype),
            pltpu.SMEM(gate_scale.shape, F32),
            pltpu.VMEM((1, width), F32),
            pltpu.VMEM((nx, 2, nh * rows, width), BF16),
            pltpu.VMEM(order + (width,), BF16),
            pltpu.VMEM((width, tokens), BF16),
            pltpu.VMEM(w_out.shape, BF16),
            pltpu.VMEM(order + (cols,), BF16),
            pltpu.VMEM(half + (cols,), F32),
            pltpu.VMEM(half + (cols - cut,), F32),
            pltpu.VMEM(half + (cut,), BF16),
            pltpu.VMEM(half + (cut,), BF16),
            pltpu.VMEM(half + (cols,), BF16),
            pltpu.VMEM(half + (cols - cut,), BF16),
            pltpu.VMEM((2,) + half + (cols,), BF16),
            pltpu.VMEM((2,) + half + (cols - cut,), BF16),
            pltpu.VMEM((nx, 2, rows, cols - cut), BF16),
            pltpu.VMEM((nx, 2, rows, cols - cut), BF16),
            pltpu.VMEM((nx, 2, rows, cols), BF16),
            pltpu.VMEM((nd, rows, cols), BF16),
            pltpu.VMEM((na, 2, nx, rows, width), BF16),
            pltpu.VMEM((na, 2, nx, rows, width), F32),
            pltpu.VMEM((na, 2, nx, rows, width), BF16),
            pltpu.VMEM((na, nx - 1, 2, rows, width), BF16),
            pltpu.VMEM((na, nx - 1, 2, rows, width), BF16),
            pltpu.VMEM((na, 2, rows, width), BF16),
            pltpu.SemaphoreType.DMA((n_sems,)),
            pltpu.SemaphoreType.DMA((n_sems,)),
            pltpu.SemaphoreType.DMA((9,)),
        ],
        compiler_params=pltpu.CompilerParams(
            collective_id=0, has_side_effects=True, vmem_limit_bytes=VMEM_LIMIT
        ),
    )(*[pltpu.with_memory_space_constraint(a, pltpu.HBM) for a in (attn_out, head_mask, gate_scale, grad_out, w_out)])
    span = cols // nd
    gw, proj, gattn = pl.pallas_call(
        weight_kernel,
        out_shape=(
            jax.ShapeDtypeStruct(w_out.shape, F32),
            jax.ShapeDtypeStruct(grad_out.shape, BF16),
            jax.ShapeDtypeStruct(attn_out.shape, BF16),
        ),
        in_specs=[vmem] * 4,
        out_specs=(hbm,) * 3,
        scratch_shapes=[
            pltpu.VMEM((2, width, span), F32),
            pltpu.SemaphoreType.DMA((2,)),
            pltpu.SemaphoreType.DMA((nd + 1,)),
        ],
        compiler_params=pltpu.CompilerParams(vmem_limit_bytes=WEIGHT_LIMIT),
    )(gt, g.reshape(tokens, cols), pj, ga.reshape(attn_out.shape))
    return proj, gattn, gw


def shards(attn_out, head_mask, gate_scale, w_out, grad_out):
    n_dp, n_head = lax.axis_size("dp"), lax.axis_size("head")
    rows, (width, cols) = grad_out.shape[0], w_out.shape
    if rows % 16 == 0 and n_dp % 2 == 0 and n_head % 2 == 0 and min(n_dp, n_head) > 2 and width % TILE == 0 and cols % (2 * TILE) == 0 and cols % (n_dp * 128) == 0 and (width // head_mask.shape[0]) % 128 == 0:
        return fused(n_head, n_dp, attn_out, head_mask, gate_scale, w_out, grad_out)
    gate_vals = head_mask.astype(jnp.float32) * gate_scale
    width_each = attn_out.shape[1] // gate_vals.shape[0]
    col_gate = jnp.repeat(gate_vals, width_each)
    gated = (attn_out.astype(jnp.float32) * col_gate[None, :]).astype(jnp.bfloat16)
    mine = lax.all_to_all(grad_out, "dp", 1, 0, tiled=True)
    every = lax.all_gather(mine.reshape(n_dp, rows, cols), "head", axis=1)
    grad_cols = every.reshape(n_dp * n_head * rows, cols)
    gated_all = lax.all_gather(gated, "dp", axis=0, tiled=True)
    part = jnp.dot(gated_all, w_out, preferred_element_type=jnp.float32).astype(jnp.bfloat16)
    summed = lax.psum_scatter(part.reshape(n_dp, n_head, rows, cols), "head", scatter_dimension=1, tiled=False)
    proj_out = lax.all_to_all(summed.reshape(n_dp * rows, cols), "dp", 0, 1, tiled=True)
    back = lax.dot_general(grad_cols, w_out, (((1,), (1,)), ((), ())), preferred_element_type=jnp.float32)
    back = lax.psum_scatter(back.astype(jnp.bfloat16), "dp", scatter_dimension=0, tiled=True)
    grad_attn = (back.astype(jnp.float32) * col_gate[None, :]).astype(jnp.bfloat16)
    grad_w = lax.dot_general(gated_all, grad_cols, (((0,), (0,)), ((), ())), preferred_element_type=jnp.float32)
    return (proj_out, grad_attn, grad_w)


def solution(mesh):
    return jax.shard_map(
        shards,
        mesh=mesh,
        in_specs=(P("dp", "head"), P("head"), P("head"), P("head", "dp"), P(("dp", "head"), None)),
        out_specs=(P(("dp", "head"), None), P("dp", "head"), P("head", "dp")),
        check_vma=False,
    )
```

```python
import functools

import jax
import jax.numpy as jnp
from jax import lax
from jax.experimental import pallas as pl
from jax.experimental.pallas import tpu as pltpu
from jax.sharding import PartitionSpec as P

MESH = pl.DeviceIdType.MESH
F32, BF16 = jnp.float32, jnp.bfloat16
TILE = 256
SHARE = 5, 8
VMEM_LIMIT = 41 * 1024 * 1024
HAND_LIMIT = 2 * 1024 * 1024
SLOTS = 3


ORDER = (
    ("gy", 0, 0), ("gz", 0, 0, 0), ("put", 0), ("proj", 0), ("sy", 2, 0), ("turn", 0), ("sb", 1, 0),
    ("gy", 0, 1), ("gz", 0, 1, 0), ("gz", 1, 0, 0), ("sy", 1, 0), ("gz", 0, 0, 1), ("gy", 1, 0), ("sb", 2, 0),
    ("gy", 1, 1), ("pass", 1), ("gz", 0, 1, 1), ("gy", 2, 0), ("gz", 1, 1, 0), ("put", 1), ("gz", 1, 0, 1),
    ("gz", 2, 0, 0), ("proj", 1), ("sb", 1, 1), ("sb", 2, 1), ("sy", 2, 1), ("gz", 2, 1, 0), ("gz", 1, 1, 1),
    ("sa", 1, 0), ("back", 1), ("sy", 1, 1), ("gy", 2, 1), ("sa", 1, 1), ("turn", 1), ("sy", 3, 1),
    ("sb", 3, 1), ("gy", 3, 0), ("cross", 1), ("back", 0), ("sa", 2, 1), ("gy", 3, 1), ("gz", 2, 0, 1),
    ("back", 2), ("ga", 1), ("sy", 3, 0), ("cross", 2), ("cross", 0), ("gz", 2, 1, 1), ("fb", 1),
    ("sy", 4, 1), ("sa", 2, 0), ("sa", 3, 1), ("sb", 3, 0), ("back", 3), ("gw", 6), ("sy", 4, 0),
    ("sa", 3, 0), ("cross", 3), ("gw", 3), ("gw", 4), ("ga", 2), ("fa", 1), ("fin", 1), ("gw", 1), ("fb", 0),
    ("ga", 0), ("gw", 5), ("gw", 2), ("ga", 3), ("gw", 7), ("fa", 0), ("fin", 0), ("gw", 0),
)


def split(cols):
    tiles = cols // TILE
    return max(1, min(tiles - 1, tiles * SHARE[0] // SHARE[1])) * TILE


def plan(na, nx, tiles):
    order = [("gz", 0, 0, 0), ("gy", 0, 0), ("put", 0), ("proj", 0)]
    for k in range(1, nx):
        order += [("gz", 0, k, 0), ("gy", 0, k)]
    order += [("gz", 0, 0, 1), ("sy", 1, 0), ("turn", 0)]
    for k in range(1, nx):
        order += [("gz", 0, k, 1), ("pass", k)]
    for k in range(1, nx):
        order += [("put", k), ("proj", k), ("sy", 1, k), ("turn", k)]
    for p in range(1, na):
        for k in range(nx):
            order += [("gz", p, k, 0)] if p < na - 1 else []
            order += [("gy", p, k), ("sb", p, k)]
            order += [("gz", p, k, 1)] if p < na - 1 else []
            order += [("sa", p, k), ("sy", p + 1, k)]
        order += [("cross", p - 2)] if p > 1 else []
        order += [("back", p - 1)]
    order += [("cross", na - 2), ("back", na - 1)]
    order += [("fb", k) for k in range(nx)] + [("fa", k) for k in range(nx)] + [("cross", na - 1)]
    order += [("fin", k) for k in reversed(range(nx))]
    order += [("gw", i) for i in range(tiles)] + [("ga", j) for j in range(na)]
    return ORDER if set(ORDER) == set(order) else order


def kernel(nh, nd, attn, mask_hbm, scale_hbm, grad, w_hbm, pj_out, ga_out, *more):
    gw_outs, more = more[:nd], more[nd:]
    (mask, scale, gate, blocks, gated, gt, w, g, pa, pb, psy, ry, sa, sb, ra, rb, fb, ryf, fin, pj,
     bs, bo, br, bs2, br2, ga, gw, ssem, rsem, lsem) = more
    na, nx = nh // 2, nd // 2
    h, d = lax.axis_index("head"), lax.axis_index("dp")
    z, b = h // 2, h % 2
    x, c = d // 2, d % 2
    rows, cols = g.shape[-2:]
    width, tokens = gt.shape
    cut = split(cols)
    first, rest = pl.ds(0, cut), pl.ds(cut, cols - cut)
    sent, ids, seen = [], {}, set()
    local, tiles = [], []

    def when(cond, fn):
        if cond is None:
            fn()
        else:
            pl.when(cond)(fn)

    def remote(key, src, dst, dev):
        i = ids.setdefault(key, len(ids))
        return pltpu.make_async_remote_copy(
            src_ref=src, dst_ref=dst, send_sem=ssem.at[i], recv_sem=rsem.at[i],
            device_id=dev, device_id_type=MESH,
        )

    def send(key, cond, make, dev):
        when(cond, lambda: remote(key, *make(), dev).start())
        sent.append((key, cond, make, dev))

    def arrive(key, ref, dev):
        remote(key, ref, ref, dev).wait_recv()

    def once(key, cond, make, dev):
        if key not in seen:
            seen.add(key)
            when(cond, lambda: arrive(key, make(), dev))

    def copy(src, dst):
        made = pltpu.make_async_copy(src, dst, lsem.at[len(local)])
        made.start()
        local.append(made)
        return len(local) - 1

    def copied(i):
        if local[i] is not None:
            local[i].wait()
            local[i] = None

    def dp(q):
        return {"head": h, "dp": q}

    def along(step):
        return {"head": (h + 2 * step + nh) % nh, "dp": d}

    beside = {"head": z * 2 + 1 - b, "dp": d}
    sibling = dp(x * 2 + 1 - c)

    def ahead(s):
        return ((x + s[0]) % nx) * 2 + (c + s[1]) % 2

    def behind(s):
        return ((x + nx - s[0]) % nx) * 2 + (c + s[1]) % 2

    far = [(kx, kc) for kx in range(1, nx) for kc in range(2)]

    def part(q):
        return grad.at[:, pl.ds(pl.multiple_of(q * cols, 128), cols)]

    own_copy = copy(part(d), g.at[0, 0, z, 0])
    attn_copy = copy(attn, blocks.at[0, 0])
    mask_copy = copy(mask_hbm, mask)
    scale_copy = copy(scale_hbm, scale)
    w_copy = copy(w_hbm, w)
    barrier = pltpu.get_barrier_semaphore()

    def greet(dev):
        pl.semaphore_signal(barrier, inc=1, device_id=dev, device_id_type=MESH)

    for s in far + [(0, 1)]:
        greet(dp(ahead(s)))
    greet(beside)
    pl.when(z > 0)(lambda: greet(along(-1)))
    pl.when(z < na - 1)(lambda: greet(along(1)))
    pl.semaphore_wait(barrier, nd + (z + na - 1) // na + (2 * na - 2 - z) // na)

    for s in far + [(0, 1)]:
        send(("swap", s), None, lambda s=s: (part(ahead(s)), g.at[0, s[0], z, s[1]]), dp(ahead(s)))
    for k in range(1, nx):
        send(("attn", k), None, lambda k=k: (attn, blocks.at[k, 0]), dp(ahead((k, 0))))
    send(("attn", 0), None, lambda: (attn, blocks.at[0, 1]), sibling)

    both = RIGHT, LEFT = 0, 1

    def unit(p, way):
        return z - p if way == RIGHT else z + p

    def held(p, way):
        return z >= p if way == RIGHT else z + p <= na - 1

    def open_to(way):
        return z < na - 1 if way == RIGHT else z > 0

    def open_from(way):
        return z > 0 if way == RIGHT else z < na - 1

    def step(way):
        return 1 if way == RIGHT else -1

    def due(p, way):
        return p > z if way == RIGHT else p > na - 1 - z

    def target(p, way):
        return na + z - p if way == RIGHT else z + p - na

    def ref_z(p, k, way, piece):
        u = unit(p, way)
        return g.at[0, k, u] if piece == 0 else g.at[1, k, u, :, :, rest]

    def ref_y(p, k, way, r):
        return g.at[r, k, z] if p == 0 else g.at[r, k, unit(p, way), :, :, first]

    def need_z(p, k, piece):
        if p:
            for way in both:
                once(("gz", p - 1, k, way, piece), held(p, way), lambda way=way: ref_z(p, k, way, piece), along(-step(way)))
        elif piece:
            need_y(0, k)
        else:
            for s in ((k, 0), (k, 1)):
                if s == (0, 0):
                    copied(own_copy)
                else:
                    once(("swap", s), None, lambda s=s: g.at[0, s[0], z, s[1]], dp(behind(s)))

    def need_y(p, k):
        for way in both if p else both[:1]:
            once(("gy", p, k, way), held(p, way) if p else None, lambda way=way: ref_y(p, k, way, 1), beside)

    def need_units(j):
        for p in range(j + 1):
            for k in range(nx):
                need_z(p, k, 0)
                need_y(p, k)
                need_z(p, k, 1)

    def tiles_of(span, fn):
        @pl.loop(0, span // TILE)
        def _(i):
            fn(pl.ds(pl.multiple_of(i * TILE, TILE), TILE))

    def gather_z(p, k, piece):
        need_z(p, k, piece)
        for way in both:
            def make(way=way):
                ref = ref_z(p, k, way, piece)
                return ref, ref
            send(("gz", p, k, way, piece), held(p, way) & open_to(way), make, along(step(way)))

    def gather_y(p, k):
        need_z(p, k, 0)
        for way in both if p else both[:1]:
            send(("gy", p, k, way), held(p, way) if p else None,
                 lambda way=way: (ref_y(p, k, way, 0), ref_y(p, k, way, 1)), beside)

    def sum_y(p, k):
        for way in both[:1] if p == na else both:
            def make(way=way):
                t = target(p, way)
                return psy.at[k, t], ry.at[k, t]
            send(("sy", p, k, way), None if p == na else due(p, way), make, beside)

    def sum_z(name, p, k):
        part_of, out, into, span = (pa, sa, ra, cut) if name == "sa" else (pb, sb, rb, cols - cut)
        for way in both:
            def run(chained, way=way):
                t = target(p, way)
                if name == "sa":
                    arrive(("sy", p, k, way), ry.at[k, t], beside)
                if chained:
                    arrive((name, p - 1, k, way), into.at[way, k, t], along(-step(way)))

                def tile(at):
                    val = part_of[k, t, ..., at]
                    if name == "sa":
                        val += ry[k, t, :, :, at].astype(F32)
                    if chained:
                        val += into[way, k, t, ..., at].astype(F32)
                    out[k, t, ..., at] = val.astype(BF16)

                tiles_of(span, tile)

            now = due(p, way)
            pl.when(now & open_from(way))(lambda: run(True))
            pl.when(now & jnp.logical_not(open_from(way)))(lambda: run(False))

            def make(way=way):
                t = target(p, way)
                return out.at[k, t], into.at[way, k, t]
            send((name, p, k, way), now, make, along(step(way)))

    def add_last(name, k):
        total, into, span = (pa, ra, cut) if name == "sa" else (pb, rb, cols - cut)
        for way in both:
            def run(way=way):
                arrive((name, na - 1, k, way), into.at[way, k, z], along(-step(way)))

                def tile(at):
                    total[k, z, ..., at] += into[way, k, z, ..., at].astype(F32)
                tiles_of(span, tile)
            pl.when(open_from(way))(run)

    def put(kx, kc):
        val = (blocks[kx, kc].astype(F32) * gate[...]).astype(BF16).reshape(na, 2, rows, width)
        for bb in range(2):
            gated[(b + bb) % 2, kx, :, kc] = val[:, bb]

    def passed(k):
        arrive(("attn", k), blocks.at[k, 0], dp(behind((k, 0))))
        send(("pass", k), None, lambda: (blocks.at[k, 0], blocks.at[k, 1]), sibling)
        make_gate()
        put(k, 0)

    def make_gate():
        if "gate" in seen:
            return
        seen.add("gate")
        copied(mask_copy)
        copied(scale_copy)
        heads = scale.shape[0]
        each = width // heads
        for i in range(heads):
            gate[:, i * each:(i + 1) * each] = jnp.full((1, each), mask[i].astype(F32) * scale[i], F32)

    def take(k):
        make_gate()
        if k:
            arrive(("pass", k), blocks.at[k, 1], sibling)
        else:
            copied(attn_copy)
            put(0, 0)
            arrive(("attn", 0), blocks.at[0, 1], sibling)
        put(k, 1)

    def turn(k):
        span = na * 2 * rows
        for r in range(2):
            lo = (r * nx + k) * span
            gt[:, lo:lo + span] = gated[r, k].reshape(span, width).T

    def project(k):
        copied(w_copy)

        def dot(at):
            lhs = gated[:, k].reshape(2 * na * 2 * rows, width)
            res = jnp.dot(lhs, w[:, at], preferred_element_type=F32)
            return res.reshape(2, na, 2, rows, TILE)

        def front(at):
            res = dot(at)
            pa[k, :, :, :, at] = res[0]
            psy[k, :, :, :, at] = res[1].astype(BF16)

        @pl.loop(cut // TILE, cols // TILE)
        def _(i):
            res = dot(pl.ds(pl.multiple_of(i * TILE, TILE), TILE))
            low = pl.ds(pl.multiple_of(i * TILE - cut, TILE), TILE)
            for r in range(2):
                pb[k, :, r, :, :, low] = res[r]

        tiles_of(cut, front)

    small = jnp.minimum(z, na - 1 - z)

    def nth(j):
        if j == 0:
            return z
        near = z - (j + 1) // 2 if j % 2 else z + (j + 1) // 2
        end = jnp.where(z == small, j, na - 1 - j)
        return jnp.where(j <= 2 * small, near, end)

    def back(j):
        need_units(j)
        copied(w_copy)
        u = nth(j)

        def tile(at):
            lhs = g[:, :, u].reshape(2 * nx * 2 * rows, cols)
            res = lax.dot_general(lhs, w[at, :], (((1,), (1,)), ((), ())), preferred_element_type=F32)
            res = res.reshape(2, nx, 2, rows, TILE)
            bs[j, :, :, :, at] = res[:, :, 1].astype(BF16)
            bo[j, :, :, :, at] = res[:, :, 0]

        tiles_of(width, tile)
        send(("pair", j), None, lambda: (bs.at[j], br.at[j]), sibling)

    def cross(j):
        arrive(("pair", j), br.at[j], sibling)
        for k in range(1, nx):
            bs2[j, k - 1] = (bo[j, :, k] + br[j, :, k].astype(F32)).astype(BF16)
            send(("cross", j, k), None, lambda k=k: (bs2.at[j, k - 1], br2.at[j, k - 1]), dp(behind((k, 0))))

    def attn_out(j):
        for k in range(1, nx):
            arrive(("cross", j, k), br2.at[j, k - 1], dp(ahead((k, 0))))
        total = bo[j, :, 0] + br[j, :, 0].astype(F32)
        for k in range(1, nx):
            total += br2[j, k - 1].astype(F32)
        total = (total * gate[...].reshape(1, 1, width)).astype(BF16)
        for r in range(2):
            ga[nth(j), (b + r) % 2] = total[r]
        copy(ga.at[nth(j)], ga_out.at[nth(j)])

    def weight(i):
        need_units(na - 1)
        slot, each = len(tiles) % SLOTS, cols // nd
        if len(tiles) >= SLOTS:
            copied(tiles[-SLOTS])
        at = slice(i * TILE, (i + 1) * TILE)
        gw[slot] = jnp.dot(gt[...], g[:, :, :, :, :, at].reshape(tokens, TILE), preferred_element_type=F32)
        lo = i * TILE % each
        tiles.append(copy(gw.at[slot], gw_outs[i * TILE // each].at[:, lo:lo + TILE]))

    def last_b(k):
        add_last("sb", k)
        fb[k] = pb[k, z, 1].astype(BF16)
        send(("fy", k), None, lambda: (fb.at[k], ryf.at[k]), beside)

    def finish(k):
        arrive(("sy", na, k, RIGHT), ry.at[k, z], beside)

        def tile(at):
            fin[k, :, :, at] = (pa[k, z, :, :, at] + ry[k, z, :, :, at].astype(F32)).astype(BF16)

        tiles_of(cut, tile)
        arrive(("fy", k), ryf.at[k], beside)
        fin[k, :, :, rest] = (pb[k, z, 0] + ryf[k].astype(F32)).astype(BF16)
        for kc in range(2):
            if (k, kc) != (0, 0):
                send(("home", (k, kc)), None, lambda kc=kc: (fin.at[k, kc], pj.at[d]), dp(behind((k, kc))))
            else:
                pj[d] = fin[0, 0]
                copy(pj.at[d], pj_out.at[d])

    steps = {
        "gz": gather_z, "gy": gather_y, "sy": sum_y, "sa": functools.partial(sum_z, "sa"),
        "sb": functools.partial(sum_z, "sb"), "pass": passed, "put": take, "proj": project, "turn": turn,
        "back": back, "cross": cross, "ga": attn_out, "gw": weight, "fb": last_b,
        "fa": functools.partial(add_last, "sa"), "fin": finish,
    }
    for name, *at in plan(na, nx, cols // TILE):
        steps[name](*at)
    for s in [(0, 1)] + far:
        arrive(("home", s), pj.at[ahead(s)], dp(ahead(s)))
        copy(pj.at[ahead(s)], pj_out.at[ahead(s)])
    for key, cond, make, dev in sent:
        when(cond, lambda: remote(key, *make(), dev).wait_send())
    for i in range(len(local)):
        copied(i)


def hand_over(pj, ga, *refs):
    *gw, proj, gattn, gw_out, sems = refs
    cols = pj.shape[2]
    each = cols // len(gw)
    pairs = [(ga, gattn)]
    for i in range(len(gw)):
        pairs.append((gw[i], gw_out.at[:, i * each:(i + 1) * each]))
        pairs.append((pj.at[i], proj.at[:, i * cols:(i + 1) * cols]))
    copies = [pltpu.make_async_copy(src, dst, sems.at[i]) for i, (src, dst) in enumerate(pairs)]
    for copy in copies:
        copy.start()
    for copy in copies:
        copy.wait()


def fused(nh, nd, attn_out, head_mask, gate_scale, w_out, grad_out):
    na, nx = nh // 2, nd // 2
    rows, cols, width = grad_out.shape[0], w_out.shape[1], w_out.shape[0]
    tokens = rows * nh * nd
    cut = split(cols)
    n_sems = 2 * nd + 4 * nx + 11 * (na + 1) * nx * 2 + na * nx
    vmem = pl.BlockSpec(memory_space=pltpu.VMEM)
    hbm = pl.BlockSpec(memory_space=pltpu.HBM)
    free = pl.BlockSpec(memory_space=pl.ANY)
    order = (2, nx, na, 2, rows)
    half = (nx, na, 2, rows)
    whole = (nx, na, 2, 2, rows)
    pj, ga, *gw = pl.pallas_call(
        functools.partial(kernel, nh, nd),
        out_shape=(
            jax.ShapeDtypeStruct((nd, rows, cols), BF16),
            jax.ShapeDtypeStruct((na, 2, rows, width), BF16),
        ) + (jax.ShapeDtypeStruct((width, cols // nd), F32),) * nd,
        in_specs=[hbm] * 5,
        out_specs=(free,) * (2 + nd),
        scratch_shapes=[
            pltpu.SMEM(head_mask.shape, head_mask.dtype),
            pltpu.SMEM(gate_scale.shape, F32),
            pltpu.VMEM((1, width), F32),
            pltpu.VMEM((nx, 2, nh * rows, width), BF16),
            pltpu.VMEM(order + (width,), BF16),
            pltpu.VMEM((width, tokens), BF16),
            pltpu.VMEM(w_out.shape, BF16),
            pltpu.VMEM(order + (cols,), BF16),
            pltpu.VMEM(half + (cut,), F32),
            pltpu.VMEM(whole + (cols - cut,), F32),
            pltpu.VMEM(half + (cut,), BF16),
            pltpu.VMEM(half + (cut,), BF16),
            pltpu.VMEM(half + (cut,), BF16),
            pltpu.VMEM(whole + (cols - cut,), BF16),
            pltpu.VMEM((2,) + half + (cut,), BF16),
            pltpu.VMEM((2,) + whole + (cols - cut,), BF16),
            pltpu.VMEM((nx, 2, rows, cols - cut), BF16),
            pltpu.VMEM((nx, 2, rows, cols - cut), BF16),
            pltpu.VMEM((nx, 2, rows, cols), BF16),
            pltpu.VMEM((nd, rows, cols), BF16),
            pltpu.VMEM((na, 2, nx, rows, width), BF16),
            pltpu.VMEM((na, 2, nx, rows, width), F32),
            pltpu.VMEM((na, 2, nx, rows, width), BF16),
            pltpu.VMEM((na, nx - 1, 2, rows, width), BF16),
            pltpu.VMEM((na, nx - 1, 2, rows, width), BF16),
            pltpu.VMEM((na, 2, rows, width), BF16),
            pltpu.VMEM((SLOTS, width, TILE), F32),
            pltpu.SemaphoreType.DMA((n_sems,)),
            pltpu.SemaphoreType.DMA((n_sems,)),
            pltpu.SemaphoreType.DMA((5 + nd + na + cols // TILE,)),
        ],
        compiler_params=pltpu.CompilerParams(
            collective_id=0, has_side_effects=True, vmem_limit_bytes=VMEM_LIMIT
        ),
    )(*[pltpu.with_memory_space_constraint(a, pltpu.HBM) for a in (attn_out, head_mask, gate_scale, grad_out, w_out)])
    proj, gattn, gw = pl.pallas_call(
        hand_over,
        out_shape=(
            jax.ShapeDtypeStruct(grad_out.shape, BF16),
            jax.ShapeDtypeStruct(attn_out.shape, BF16),
            jax.ShapeDtypeStruct(w_out.shape, F32),
        ),
        in_specs=[vmem] * (2 + nd),
        out_specs=(hbm,) * 3,
        scratch_shapes=[pltpu.SemaphoreType.DMA((2 * nd + 1,))],
        compiler_params=pltpu.CompilerParams(vmem_limit_bytes=HAND_LIMIT),
    )(pj, ga.reshape(attn_out.shape), *gw)
    return proj, gattn, gw


def shards(attn_out, head_mask, gate_scale, w_out, grad_out):
    n_dp, n_head = lax.axis_size("dp"), lax.axis_size("head")
    rows, (width, cols) = grad_out.shape[0], w_out.shape
    if rows % 16 == 0 and n_dp % 2 == 0 and n_head % 2 == 0 and min(n_dp, n_head) > 2 and width % TILE == 0 and cols % (2 * TILE) == 0 and cols % (n_dp * 128) == 0 and (width // head_mask.shape[0]) % 128 == 0:
        return fused(n_head, n_dp, attn_out, head_mask, gate_scale, w_out, grad_out)
    gate_vals = head_mask.astype(jnp.float32) * gate_scale
    width_each = attn_out.shape[1] // gate_vals.shape[0]
    col_gate = jnp.repeat(gate_vals, width_each)
    gated = (attn_out.astype(jnp.float32) * col_gate[None, :]).astype(jnp.bfloat16)
    mine = lax.all_to_all(grad_out, "dp", 1, 0, tiled=True)
    every = lax.all_gather(mine.reshape(n_dp, rows, cols), "head", axis=1)
    grad_cols = every.reshape(n_dp * n_head * rows, cols)
    gated_all = lax.all_gather(gated, "dp", axis=0, tiled=True)
    part = jnp.dot(gated_all, w_out, preferred_element_type=jnp.float32).astype(jnp.bfloat16)
    summed = lax.psum_scatter(part.reshape(n_dp, n_head, rows, cols), "head", scatter_dimension=1, tiled=False)
    proj_out = lax.all_to_all(summed.reshape(n_dp * rows, cols), "dp", 0, 1, tiled=True)
    back = lax.dot_general(grad_cols, w_out, (((1,), (1,)), ((), ())), preferred_element_type=jnp.float32)
    back = lax.psum_scatter(back.astype(jnp.bfloat16), "dp", scatter_dimension=0, tiled=True)
    grad_attn = (back.astype(jnp.float32) * col_gate[None, :]).astype(jnp.bfloat16)
    grad_w = lax.dot_general(gated_all, grad_cols, (((0,), (0,)), ((), ())), preferred_element_type=jnp.float32)
    return (proj_out, grad_attn, grad_w)


def solution(mesh):
    return jax.shard_map(
        shards,
        mesh=mesh,
        in_specs=(P("dp", "head"), P("head"), P("head"), P("head", "dp"), P(("dp", "head"), None)),
        out_specs=(P(("dp", "head"), None), P("dp", "head"), P("head", "dp")),
        check_vma=False,
    )
```

```python
import functools

import jax
import jax.numpy as jnp
from jax import lax
from jax.experimental import pallas as pl
from jax.experimental.pallas import tpu as pltpu
from jax.sharding import PartitionSpec as P

MESH = pl.DeviceIdType.MESH
F32, BF16 = jnp.float32, jnp.bfloat16
TILE = 256
SUM_SHARE = 5, 8
GATHER_SHARE = 9, 16
VMEM_LIMIT = 41 * 1024 * 1024
HAND_LIMIT = 2 * 1024 * 1024
SLOTS = 3


ORDER = (
    ("oy", 0, 1), ("oz", 0, 1), ("put", 0), ("oy", 1, 0), ("oz", 1, 0), ("oz", 1, 1), ("oy", 1, 1),
    ("gy", 1, 0), ("gz", 0, 0, 1), ("proj", 0), ("gz", 1, 0, 0), ("sy", 1, 0), ("turn", 0), ("sb", 1, 0),
    ("gz", 0, 1, 1), ("back", 0), ("gy", 1, 1), ("gz", 1, 1, 0), ("sy", 2, 0), ("sb", 2, 0), ("pass", 1),
    ("sa", 1, 0), ("put", 1), ("gz", 2, 0, 0), ("gy", 2, 0), ("proj", 1), ("sy", 1, 1), ("gz", 1, 1, 1),
    ("sy", 2, 1), ("sb", 1, 1), ("back", 1), ("sa", 1, 1), ("gy", 2, 1), ("gz", 1, 0, 1), ("cross", 1),
    ("gy", 3, 0), ("sb", 2, 1), ("cross", 0), ("gz", 2, 1, 0), ("sy", 3, 1), ("gz", 2, 1, 1), ("sa", 2, 1),
    ("sa", 2, 0), ("gz", 2, 0, 1), ("ga", 1), ("back", 2), ("gy", 3, 1), ("sy", 3, 0), ("sb", 3, 1),
    ("cross", 2), ("turn", 1), ("ga", 0), ("sy", 4, 1), ("sa", 3, 1), ("sb", 3, 0), ("back", 3), ("gw", 7),
    ("ga", 2), ("fb", 1), ("cross", 3), ("gw", 6), ("sa", 3, 0), ("sy", 4, 0), ("gw", 5), ("fa", 1),
    ("fin", 1), ("gw", 3), ("ga", 3), ("fb", 0), ("gw", 0), ("gw", 1), ("gw", 4), ("fa", 0), ("fin", 0),
    ("gw", 2),
)


def split(cols, share, tile):
    tiles = cols // tile
    return max(1, min(tiles - 1, tiles * share[0] // share[1])) * tile


def plan(na, nx, tiles):
    order = [("oz", 0, 1), ("oy", 0, 1), ("put", 0), ("proj", 0)]
    for k in range(1, nx):
        order += [(name, k, kc) for kc in range(2) for name in ("oz", "oy")]
    order += [("gz", 0, 0, 1), ("sy", 1, 0), ("turn", 0)]
    for k in range(1, nx):
        order += [("gz", 0, k, 1), ("pass", k)]
    for k in range(1, nx):
        order += [("put", k), ("proj", k), ("sy", 1, k), ("turn", k)]
    for p in range(1, na):
        for k in range(nx):
            order += [("gz", p, k, 0)] if p < na - 1 else []
            order += [("gy", p, k), ("sb", p, k)]
            order += [("gz", p, k, 1)] if p < na - 1 else []
            order += [("sa", p, k), ("sy", p + 1, k)]
        order += [("cross", p - 2)] if p > 1 else []
        order += [("back", p - 1)]
    order += [("cross", na - 2), ("back", na - 1)]
    order += [("fb", k) for k in range(nx)] + [("fa", k) for k in range(nx)] + [("cross", na - 1)]
    order += [("fin", k) for k in reversed(range(nx))]
    order += [("gw", i) for i in range(tiles)] + [("ga", j) for j in range(na)]
    return ORDER if set(ORDER) == set(order) else order


def semaphores(na, nx, tiles):
    each = {"oz": 2, "oy": 1, "gz": 2, "gy": 2, "sy": 2, "sa": 2, "sb": 2, "pass": 1, "back": 1,
            "cross": nx - 1, "fb": 1, "fin": 2}
    return 3 + 2 * nx + nx + sum(each.get(step[0], 0) for step in plan(na, nx, tiles))


def kernel(nh, nd, attn, mask_hbm, scale_hbm, grad, w_hbm, pj_out, ga_out, *more):
    gw_outs, more = more[:nd], more[nd:]
    (mask, scale, gate, blocks, gated, gt, w, g, pa, pb, psy, ry, sa, sb, ra, rb, fb, ryf, fin, pj,
     bs, bo, br, bs2, br2, ga, gw, ssem, rsem, lsem) = more
    na, nx = nh // 2, nd // 2
    h, d = lax.axis_index("head"), lax.axis_index("dp")
    z, b = h // 2, h % 2
    x, c = d // 2, d % 2
    rows, cols = g.shape[-2:]
    width, tokens = gt.shape
    cut, mid = split(cols, SUM_SHARE, TILE), split(cols, GATHER_SHARE, 128)
    first, rest = pl.ds(0, mid), pl.ds(mid, cols - mid)
    sent, ids, seen = [], {}, set()
    local, tiles = [], []

    def when(cond, fn):
        if cond is None:
            fn()
        else:
            pl.when(cond)(fn)

    def remote(key, src, dst, dev):
        if key[0] in ("gz", "sa", "sb"):
            key = ("z", *key[1:4], key[4] if key[0] == "gz" else int(key[0] == "sb"))
        i = ids.setdefault(key, len(ids))
        return pltpu.make_async_remote_copy(
            src_ref=src, dst_ref=dst, send_sem=ssem.at[0], recv_sem=rsem.at[i],
            device_id=dev, device_id_type=MESH,
        )

    def send(key, cond, make, dev):
        when(cond, lambda: remote(key, *make(), dev).start())
        sent.append((key, cond, make, dev))

    def arrive(key, ref, dev):
        remote(key, ref, ref, dev).wait_recv()

    def once(key, cond, make, dev):
        if key not in seen:
            seen.add(key)
            when(cond, lambda: arrive(key, make(), dev))

    def copy(src, dst):
        made = pltpu.make_async_copy(src, dst, lsem.at[len(local)])
        made.start()
        local.append(made)
        return len(local) - 1

    def copied(i):
        if local[i] is not None:
            local[i].wait()
            local[i] = None

    def dp(q):
        return {"head": h, "dp": q}

    def along(step):
        return {"head": (h + 2 * step + nh) % nh, "dp": d}

    beside = {"head": z * 2 + 1 - b, "dp": d}
    sibling = dp(x * 2 + 1 - c)

    def ahead(s):
        return ((x + s[0]) % nx) * 2 + (c + s[1]) % 2

    def behind(s):
        return ((x + nx - s[0]) % nx) * 2 + (c + s[1]) % 2

    far = [(kx, kc) for kx in range(1, nx) for kc in range(2)]

    def part(q):
        return grad.at[:, pl.ds(pl.multiple_of(q * cols, 128), cols)]

    own_copy = copy(part(d), g.at[0, 0, z, 0])
    attn_copy = copy(attn, blocks.at[0, 0])
    mask_copy = copy(mask_hbm, mask)
    scale_copy = copy(scale_hbm, scale)
    w_copy = copy(w_hbm, w)
    barrier = pltpu.get_barrier_semaphore()

    def greet(dev):
        pl.semaphore_signal(barrier, inc=1, device_id=dev, device_id_type=MESH)

    for s in far + [(0, 1)]:
        greet(dp(ahead(s)))
    greet(beside)
    pl.when(z > 0)(lambda: greet(along(-1)))
    pl.when(z < na - 1)(lambda: greet(along(1)))
    pl.semaphore_wait(barrier, nd + (z + na - 1) // na + (2 * na - 2 - z) // na)

    both = RIGHT, LEFT = 0, 1

    def open_to(way):
        return z < na - 1 if way == RIGHT else z > 0

    def open_from(way):
        return z > 0 if way == RIGHT else z < na - 1

    def step(way):
        return 1 if way == RIGHT else -1

    def offer_z(k, kc):
        need_own(k, kc)
        src = g.at[0, k, z, kc] if k or kc else part(d)
        for way in both:
            send(("oz", k, kc, way), open_to(way), lambda: (src, g.at[0, k, z, kc]), along(step(way)))

    def offer_y(k, kc):
        need_own(k, kc)
        src = g.at[0, k, z, kc] if k or kc else part(d)
        send(("oy", k, kc), None, lambda: (src, g.at[1, k, z, kc]), beside)

    def need_own(k, kc):
        if k or kc:
            once(("swap", (k, kc)), None, lambda: g.at[0, k, z, kc], dp(behind((k, kc))))

    offer_z(0, 0)
    offer_y(0, 0)
    for s in far + [(0, 1)]:
        send(("swap", s), None, lambda s=s: (part(ahead(s)), g.at[0, s[0], z, s[1]]), dp(ahead(s)))
    for k in range(1, nx):
        send(("attn", k), None, lambda k=k: (attn, blocks.at[k, 0]), dp(ahead((k, 0))))
    send(("attn", 0), None, lambda: (attn, blocks.at[0, 1]), sibling)

    def unit(p, way):
        return z - p if way == RIGHT else z + p

    def held(p, way):
        return z >= p if way == RIGHT else z + p <= na - 1

    def due(p, way):
        return p > z if way == RIGHT else p > na - 1 - z

    def target(p, way):
        return na + z - p if way == RIGHT else z + p - na

    def ref_z(p, k, way, piece):
        u = unit(p, way)
        return g.at[0, k, u] if piece == 0 else g.at[1, k, u, :, :, rest]

    def ref_y(p, k, way, r):
        return g.at[r, k, unit(p, way), :, :, first]

    def need_z(p, k, piece):
        if p == 0 and piece:
            need_y(0, k)
        elif p == 0:
            if k == 0:
                copied(own_copy)
            need_own(k, 0)
            need_own(k, 1)
        for way in both if p else ():
            if p == 1 and piece == 0:
                for kc in range(2):
                    once(("oz", k, kc, way), held(p, way), lambda: g.at[0, k, unit(p, way), kc], along(-step(way)))
            else:
                once(("gz", p - 1, k, way, piece), held(p, way), lambda: ref_z(p, k, way, piece), along(-step(way)))

    def need_y(p, k):
        if p == 0:
            for kc in range(2):
                once(("oy", k, kc), None, lambda: g.at[1, k, z, kc], beside)
        for way in both if p else ():
            once(("gy", p, k, way), held(p, way), lambda: ref_y(p, k, way, 1), beside)

    def need_units(j):
        for p in range(j + 1):
            for k in range(nx):
                need_z(p, k, 0)
                need_y(p, k)
                need_z(p, k, 1)

    def tiles_of(span, fn):
        @pl.loop(0, span // TILE)
        def _(i):
            fn(pl.ds(pl.multiple_of(i * TILE, TILE), TILE))

    def gather_z(p, k, piece):
        need_z(p, k, piece)
        for way in both:
            def make(way=way):
                ref = ref_z(p, k, way, piece)
                return ref, ref
            send(("gz", p, k, way, piece), held(p, way) & open_to(way), make, along(step(way)))

    def gather_y(p, k):
        need_z(p, k, 0)
        for way in both:
            send(("gy", p, k, way), held(p, way),
                 lambda way=way: (ref_y(p, k, way, 0), ref_y(p, k, way, 1)), beside)

    def sum_y(p, k):
        for way in both[:1] if p == na else both:
            def make(way=way):
                t = target(p, way)
                return psy.at[k, t], ry.at[k, t]
            send(("sy", p, k, way), None if p == na else due(p, way), make, beside)

    def sum_z(name, p, k):
        part_of, out, into, span = (pa, sa, ra, cut) if name == "sa" else (pb, sb, rb, cols - cut)
        for way in both:
            def run(chained, way=way):
                t = target(p, way)
                if name == "sa":
                    arrive(("sy", p, k, way), ry.at[k, t], beside)
                if chained:
                    arrive((name, p - 1, k, way), into.at[way, k, t], along(-step(way)))

                def tile(at):
                    val = part_of[k, t, ..., at]
                    if name == "sa":
                        val += ry[k, t, :, :, at].astype(F32)
                    if chained:
                        val += into[way, k, t, ..., at].astype(F32)
                    out[k, t, ..., at] = val.astype(BF16)

                tiles_of(span, tile)

            now = due(p, way)
            pl.when(now & open_from(way))(lambda: run(True))
            pl.when(now & jnp.logical_not(open_from(way)))(lambda: run(False))

            def make(way=way):
                t = target(p, way)
                return out.at[k, t], into.at[way, k, t]
            send((name, p, k, way), now, make, along(step(way)))

    def add_last(name, k):
        total, into, span = (pa, ra, cut) if name == "sa" else (pb, rb, cols - cut)
        for way in both:
            def run(way=way):
                arrive((name, na - 1, k, way), into.at[way, k, z], along(-step(way)))

                def tile(at):
                    total[k, z, ..., at] += into[way, k, z, ..., at].astype(F32)
                tiles_of(span, tile)
            pl.when(open_from(way))(run)

    def put(kx, kc):
        val = (blocks[kx, kc].astype(F32) * gate[...]).astype(BF16).reshape(na, 2, rows, width)
        for bb in range(2):
            gated[(b + bb) % 2, kx, :, kc] = val[:, bb]

    def passed(k):
        arrive(("attn", k), blocks.at[k, 0], dp(behind((k, 0))))
        send(("pass", k), None, lambda: (blocks.at[k, 0], blocks.at[k, 1]), sibling)
        make_gate()
        put(k, 0)

    def make_gate():
        if "gate" in seen:
            return
        seen.add("gate")
        copied(mask_copy)
        copied(scale_copy)
        heads = scale.shape[0]
        each = width // heads
        for i in range(heads):
            gate[:, i * each:(i + 1) * each] = jnp.full((1, each), mask[i].astype(F32) * scale[i], F32)

    def take(k):
        make_gate()
        if k:
            arrive(("pass", k), blocks.at[k, 1], sibling)
        else:
            copied(attn_copy)
            put(0, 0)
            arrive(("attn", 0), blocks.at[0, 1], sibling)
        put(k, 1)

    def turn(k):
        span = na * 2 * rows
        for r in range(2):
            lo = (r * nx + k) * span
            gt[:, lo:lo + span] = gated[r, k].reshape(span, width).T

    def project(k):
        copied(w_copy)

        def dot(at):
            lhs = gated[:, k].reshape(2 * na * 2 * rows, width)
            res = jnp.dot(lhs, w[:, at], preferred_element_type=F32)
            return res.reshape(2, na, 2, rows, TILE)

        def front(at):
            res = dot(at)
            pa[k, :, :, :, at] = res[0]
            psy[k, :, :, :, at] = res[1].astype(BF16)

        @pl.loop(cut // TILE, cols // TILE)
        def _(i):
            res = dot(pl.ds(pl.multiple_of(i * TILE, TILE), TILE))
            low = pl.ds(pl.multiple_of(i * TILE - cut, TILE), TILE)
            for r in range(2):
                pb[k, :, r, :, :, low] = res[r]

        tiles_of(cut, front)

    small = jnp.minimum(z, na - 1 - z)

    def nth(j):
        if j == 0:
            return z
        near = z - (j + 1) // 2 if j % 2 else z + (j + 1) // 2
        end = jnp.where(z == small, j, na - 1 - j)
        return jnp.where(j <= 2 * small, near, end)

    def back(j):
        need_units(j)
        copied(w_copy)
        u = nth(j)

        def tile(at):
            lhs = g[:, :, u].reshape(2 * nx * 2 * rows, cols)
            res = lax.dot_general(lhs, w[at, :], (((1,), (1,)), ((), ())), preferred_element_type=F32)
            res = res.reshape(2, nx, 2, rows, TILE)
            bs[j, :, :, :, at] = res[:, :, 1].astype(BF16)
            bo[j, :, :, :, at] = res[:, :, 0]

        tiles_of(width, tile)
        send(("pair", j), None, lambda: (bs.at[j], br.at[j]), sibling)

    def cross(j):
        arrive(("pair", j), br.at[j], sibling)
        for k in range(1, nx):
            bs2[j, k - 1] = (bo[j, :, k] + br[j, :, k].astype(F32)).astype(BF16)
            send(("cross", j, k), None, lambda k=k: (bs2.at[j, k - 1], br2.at[j, k - 1]), dp(behind((k, 0))))

    def attn_out(j):
        for k in range(1, nx):
            arrive(("cross", j, k), br2.at[j, k - 1], dp(ahead((k, 0))))
        total = bo[j, :, 0] + br[j, :, 0].astype(F32)
        for k in range(1, nx):
            total += br2[j, k - 1].astype(F32)
        total = (total * gate[...].reshape(1, 1, width)).astype(BF16)
        for r in range(2):
            ga[nth(j), (b + r) % 2] = total[r]
        copy(ga.at[nth(j)], ga_out.at[nth(j)])

    def weight(i):
        need_units(na - 1)
        slot, each = len(tiles) % SLOTS, cols // nd
        if len(tiles) >= SLOTS:
            copied(tiles[-SLOTS])
        at = slice(i * TILE, (i + 1) * TILE)
        gw[slot] = jnp.dot(gt[...], g[:, :, :, :, :, at].reshape(tokens, TILE), preferred_element_type=F32)
        lo = i * TILE % each
        tiles.append(copy(gw.at[slot], gw_outs[i * TILE // each].at[:, lo:lo + TILE]))

    def last_b(k):
        add_last("sb", k)
        fb[k] = pb[k, z, 1].astype(BF16)
        send(("fy", k), None, lambda: (fb.at[k], ryf.at[k]), beside)

    def finish(k):
        arrive(("sy", na, k, RIGHT), ry.at[k, z], beside)

        def tile(at):
            fin[k, :, :, at] = (pa[k, z, :, :, at] + ry[k, z, :, :, at].astype(F32)).astype(BF16)

        tiles_of(cut, tile)
        arrive(("fy", k), ryf.at[k], beside)
        fin[k, :, :, cut:] = (pb[k, z, 0] + ryf[k].astype(F32)).astype(BF16)
        for kc in range(2):
            if (k, kc) != (0, 0):
                send(("home", (k, kc)), None, lambda kc=kc: (fin.at[k, kc], pj.at[d]), dp(behind((k, kc))))
            else:
                pj[d] = fin[0, 0]
                copy(pj.at[d], pj_out.at[d])

    steps = {
        "oz": offer_z, "oy": offer_y, "gz": gather_z, "gy": gather_y, "sy": sum_y, "sa": functools.partial(sum_z, "sa"),
        "sb": functools.partial(sum_z, "sb"), "pass": passed, "put": take, "proj": project, "turn": turn,
        "back": back, "cross": cross, "ga": attn_out, "gw": weight, "fb": last_b,
        "fa": functools.partial(add_last, "sa"), "fin": finish,
    }
    for name, *at in plan(na, nx, cols // TILE):
        steps[name](*at)
    for s in [(0, 1)] + far:
        arrive(("home", s), pj.at[ahead(s)], dp(ahead(s)))
        copy(pj.at[ahead(s)], pj_out.at[ahead(s)])
    for key, cond, make, dev in sent:
        when(cond, lambda: remote(key, *make(), dev).wait_send())
    for i in range(len(local)):
        copied(i)


def hand_over(pj, ga, *refs):
    *gw, proj, gattn, gw_out, sems = refs
    cols = pj.shape[2]
    each = cols // len(gw)
    pairs = [(ga, gattn)]
    for i in range(len(gw)):
        pairs.append((gw[i], gw_out.at[:, i * each:(i + 1) * each]))
        pairs.append((pj.at[i], proj.at[:, i * cols:(i + 1) * cols]))
    copies = [pltpu.make_async_copy(src, dst, sems.at[i]) for i, (src, dst) in enumerate(pairs)]
    for copy in copies:
        copy.start()
    for copy in copies:
        copy.wait()


def fused(nh, nd, attn_out, head_mask, gate_scale, w_out, grad_out):
    na, nx = nh // 2, nd // 2
    rows, cols, width = grad_out.shape[0], w_out.shape[1], w_out.shape[0]
    tokens = rows * nh * nd
    cut = split(cols, SUM_SHARE, TILE)
    n_sems = semaphores(na, nx, cols // TILE)
    vmem = pl.BlockSpec(memory_space=pltpu.VMEM)
    hbm = pl.BlockSpec(memory_space=pltpu.HBM)
    free = pl.BlockSpec(memory_space=pl.ANY)
    order = (2, nx, na, 2, rows)
    half = (nx, na, 2, rows)
    whole = (nx, na, 2, 2, rows)
    pj, ga, *gw = pl.pallas_call(
        functools.partial(kernel, nh, nd),
        out_shape=(
            jax.ShapeDtypeStruct((nd, rows, cols), BF16),
            jax.ShapeDtypeStruct((na, 2, rows, width), BF16),
        ) + (jax.ShapeDtypeStruct((width, cols // nd), F32),) * nd,
        in_specs=[hbm] * 5,
        out_specs=(free,) * (2 + nd),
        scratch_shapes=[
            pltpu.SMEM(head_mask.shape, head_mask.dtype),
            pltpu.SMEM(gate_scale.shape, F32),
            pltpu.VMEM((1, width), F32),
            pltpu.VMEM((nx, 2, nh * rows, width), BF16),
            pltpu.VMEM(order + (width,), BF16),
            pltpu.VMEM((width, tokens), BF16),
            pltpu.VMEM(w_out.shape, BF16),
            pltpu.VMEM(order + (cols,), BF16),
            pltpu.VMEM(half + (cut,), F32),
            pltpu.VMEM(whole + (cols - cut,), F32),
            pltpu.VMEM(half + (cut,), BF16),
            pltpu.VMEM(half + (cut,), BF16),
            pltpu.VMEM(half + (cut,), BF16),
            pltpu.VMEM(whole + (cols - cut,), BF16),
            pltpu.VMEM((2,) + half + (cut,), BF16),
            pltpu.VMEM((2,) + whole + (cols - cut,), BF16),
            pltpu.VMEM((nx, 2, rows, cols - cut), BF16),
            pltpu.VMEM((nx, 2, rows, cols - cut), BF16),
            pltpu.VMEM((nx, 2, rows, cols), BF16),
            pltpu.VMEM((nd, rows, cols), BF16),
            pltpu.VMEM((na, 2, nx, rows, width), BF16),
            pltpu.VMEM((na, 2, nx, rows, width), F32),
            pltpu.VMEM((na, 2, nx, rows, width), BF16),
            pltpu.VMEM((na, nx - 1, 2, rows, width), BF16),
            pltpu.VMEM((na, nx - 1, 2, rows, width), BF16),
            pltpu.VMEM((na, 2, rows, width), BF16),
            pltpu.VMEM((SLOTS, width, TILE), F32),
            pltpu.SemaphoreType.DMA((1,)),
            pltpu.SemaphoreType.DMA((n_sems,)),
            pltpu.SemaphoreType.DMA((5 + nd + na + cols // TILE,)),
        ],
        compiler_params=pltpu.CompilerParams(
            collective_id=0, has_side_effects=True, vmem_limit_bytes=VMEM_LIMIT
        ),
    )(*[pltpu.with_memory_space_constraint(a, pltpu.HBM) for a in (attn_out, head_mask, gate_scale, grad_out, w_out)])
    proj, gattn, gw = pl.pallas_call(
        hand_over,
        out_shape=(
            jax.ShapeDtypeStruct(grad_out.shape, BF16),
            jax.ShapeDtypeStruct(attn_out.shape, BF16),
            jax.ShapeDtypeStruct(w_out.shape, F32),
        ),
        in_specs=[vmem] * (2 + nd),
        out_specs=(hbm,) * 3,
        scratch_shapes=[pltpu.SemaphoreType.DMA((2 * nd + 1,))],
        compiler_params=pltpu.CompilerParams(vmem_limit_bytes=HAND_LIMIT),
    )(pj, ga.reshape(attn_out.shape), *gw)
    return proj, gattn, gw


def shards(attn_out, head_mask, gate_scale, w_out, grad_out):
    n_dp, n_head = lax.axis_size("dp"), lax.axis_size("head")
    rows, (width, cols) = grad_out.shape[0], w_out.shape
    if rows % 16 == 0 and n_dp % 2 == 0 and n_head % 2 == 0 and min(n_dp, n_head) > 2 and width % TILE == 0 and cols % (2 * TILE) == 0 and cols % (n_dp * 128) == 0 and (width // head_mask.shape[0]) % 128 == 0:
        return fused(n_head, n_dp, attn_out, head_mask, gate_scale, w_out, grad_out)
    gate_vals = head_mask.astype(jnp.float32) * gate_scale
    width_each = attn_out.shape[1] // gate_vals.shape[0]
    col_gate = jnp.repeat(gate_vals, width_each)
    gated = (attn_out.astype(jnp.float32) * col_gate[None, :]).astype(jnp.bfloat16)
    mine = lax.all_to_all(grad_out, "dp", 1, 0, tiled=True)
    every = lax.all_gather(mine.reshape(n_dp, rows, cols), "head", axis=1)
    grad_cols = every.reshape(n_dp * n_head * rows, cols)
    gated_all = lax.all_gather(gated, "dp", axis=0, tiled=True)
    part = jnp.dot(gated_all, w_out, preferred_element_type=jnp.float32).astype(jnp.bfloat16)
    summed = lax.psum_scatter(part.reshape(n_dp, n_head, rows, cols), "head", scatter_dimension=1, tiled=False)
    proj_out = lax.all_to_all(summed.reshape(n_dp * rows, cols), "dp", 0, 1, tiled=True)
    back = lax.dot_general(grad_cols, w_out, (((1,), (1,)), ((), ())), preferred_element_type=jnp.float32)
    back = lax.psum_scatter(back.astype(jnp.bfloat16), "dp", scatter_dimension=0, tiled=True)
    grad_attn = (back.astype(jnp.float32) * col_gate[None, :]).astype(jnp.bfloat16)
    grad_w = lax.dot_general(gated_all, grad_cols, (((0,), (0,)), ((), ())), preferred_element_type=jnp.float32)
    return (proj_out, grad_attn, grad_w)


def solution(mesh):
    return jax.shard_map(
        shards,
        mesh=mesh,
        in_specs=(P("dp", "head"), P("head"), P("head"), P("head", "dp"), P(("dp", "head"), None)),
        out_specs=(P(("dp", "head"), None), P("dp", "head"), P("head", "dp")),
        check_vma=False,
    )
```

```python
import functools

import jax
import jax.numpy as jnp
from jax import lax
from jax.experimental import pallas as pl
from jax.experimental.pallas import tpu as pltpu
from jax.sharding import PartitionSpec as P

MESH = pl.DeviceIdType.MESH
F32, BF16 = jnp.float32, jnp.bfloat16
TILE = 256
SUM_SHARE = 5, 8
GATHER_SHARE = 9, 16
VMEM_LIMIT = 41 * 1024 * 1024
HAND_LIMIT = 2 * 1024 * 1024
SLOTS = 3


ORDER = (
    ("oy", 0, 1), ("oz", 0, 1), ("put", 0), ("oy", 1, 0), ("turn", 0), ("oz", 1, 0), ("oy", 1, 1),
    ("oz", 1, 1), ("gz", 0, 0, 1), ("proj", 0), ("gz", 1, 0, 0), ("sy", 1, 0), ("sy", 2, 0), ("gz", 0, 1, 1),
    ("gz", 1, 1, 0), ("gy", 1, 0), ("back", 0), ("sb", 1, 0), ("gy", 1, 1), ("pass", 1), ("sa", 1, 0),
    ("sb", 2, 0), ("put", 1), ("gz", 2, 0, 0), ("gz", 1, 0, 1), ("proj", 1), ("gz", 1, 1, 1), ("sy", 1, 1),
    ("sy", 2, 1), ("gy", 2, 0), ("sb", 1, 1), ("cross", 0), ("gz", 2, 1, 0), ("gy", 2, 1), ("turn", 1),
    ("sa", 1, 1), ("sb", 2, 1), ("sy", 3, 1), ("sa", 2, 1), ("gy", 3, 0), ("gz", 2, 0, 1), ("sa", 2, 0),
    ("gz", 2, 1, 1), ("back", 2), ("sb", 3, 1), ("gy", 3, 1), ("sy", 3, 0), ("cross", 2), ("back", 1),
    ("ga", 0), ("sy", 4, 1), ("cross", 1), ("sa", 3, 1), ("back", 3), ("gw", 7), ("sb", 3, 0), ("cross", 3),
    ("fb", 1), ("gw", 3), ("gw", 5), ("sy", 4, 0), ("gw", 6), ("fa", 1), ("gw", 2), ("fin", 1), ("sa", 3, 0),
    ("gw", 0), ("fb", 0), ("sc", 3, 0), ("ga", 1), ("gw", 1), ("ga", 2), ("fa", 0), ("gw", 4), ("fin", 0),
    ("fc", 0), ("ga", 3), ("fic", 0),
)


def split(cols, share, tile):
    tiles = cols // tile
    return max(1, min(tiles - 1, tiles * share[0] // share[1])) * tile


def plan(na, nx, tiles):
    order = [("oz", 0, 1), ("oy", 0, 1), ("put", 0), ("proj", 0)]
    for k in range(1, nx):
        order += [(name, k, kc) for kc in range(2) for name in ("oz", "oy")]
    order += [("gz", 0, 0, 1), ("sy", 1, 0), ("turn", 0)]
    for k in range(1, nx):
        order += [("gz", 0, k, 1), ("pass", k)]
    for k in range(1, nx):
        order += [("put", k), ("proj", k), ("sy", 1, k), ("turn", k)]
    for p in range(1, na):
        for k in range(nx):
            order += [("gz", p, k, 0)] if p < na - 1 else []
            order += [("gy", p, k), ("sb", p, k)]
            order += [("gz", p, k, 1)] if p < na - 1 else []
            order += [("sa", p, k), ("sy", p + 1, k)]
        order += [("sc", p, 0)] if p == na - 1 else []
        order += [("cross", p - 2)] if p > 1 else []
        order += [("back", p - 1)]
    order += [("cross", na - 2), ("back", na - 1)]
    order += [("fb", k) for k in range(nx)] + [("fa", k) for k in range(nx)] + [("cross", na - 1)]
    order += [("fin", k) for k in reversed(range(nx))] + [("fc", 0), ("fic", 0)]
    order += [("gw", i) for i in range(tiles)] + [("ga", j) for j in range(na)]
    return ORDER if set(ORDER) == set(order) else order


def semaphores(na, nx, tiles):
    each = {"oz": 2, "oy": 1, "sy": 2, "sa": 2, "sb": 2, "sc": 2, "pass": 1, "back": 1, "cross": nx - 1, "fb": 1, "fin": 2}
    return 3 + 2 * nx + nx + 2 * nx + sum(each.get(step[0], 0) for step in plan(na, nx, tiles))


def kernel(nh, nd, attn, mask_hbm, scale_hbm, grad, w_hbm, pj_out, ga_out, *more):
    gw_outs, more = more[:nd], more[nd:]
    (mask, scale, gate, blocks, gated, gt, w, g, pa, pb, psy, ry, sa, sb, ra, rb, fb, ryf, fin,
     bs, bo, br, bs2, br2, ga, gw, ssem, rsem, lsem) = more
    na, nx = nh // 2, nd // 2
    h, d = lax.axis_index("head"), lax.axis_index("dp")
    z, b = h // 2, h % 2
    x, c = d // 2, d % 2
    rows, cols = g.shape[-2:]
    width, tokens = gt.shape
    cut, mid = split(cols, SUM_SHARE, TILE), split(cols, GATHER_SHARE, 128)
    first, rest = pl.ds(0, mid), pl.ds(mid, cols - mid)
    sent, ids, seen = [], {}, set()
    local, tiles = [], []

    def when(cond, fn):
        if cond is None:
            fn()
        else:
            pl.when(cond)(fn)

    def remote(key, src, dst, dev):
        if key[0] in ("gz", "sa", "sb"):
            key = ("z", *key[1:4], key[4] if key[0] == "gz" else int(key[0] == "sb"))
        if key[0] in ("gy", "sy"):
            key = ("y", *key[1:])
        i = ids.setdefault(key, len(ids))
        return pltpu.make_async_remote_copy(
            src_ref=src, dst_ref=dst, send_sem=ssem.at[0], recv_sem=rsem.at[i],
            device_id=dev, device_id_type=MESH,
        )

    def send(key, cond, make, dev):
        when(cond, lambda: remote(key, *make(), dev).start())
        sent.append((key, cond, make, dev))

    def arrive(key, ref, dev):
        remote(key, ref, ref, dev).wait_recv()

    def once(key, cond, make, dev):
        if key not in seen:
            seen.add(key)
            when(cond, lambda: arrive(key, make(), dev))

    def copy(src, dst):
        made = pltpu.make_async_copy(src, dst, lsem.at[len(local)])
        made.start()
        local.append(made)
        return len(local) - 1

    def copied(i):
        if local[i] is not None:
            local[i].wait()
            local[i] = None

    def dp(q):
        return {"head": h, "dp": q}

    def along(step):
        return {"head": (h + 2 * step + nh) % nh, "dp": d}

    beside = {"head": z * 2 + 1 - b, "dp": d}
    sibling = dp(x * 2 + 1 - c)

    def ahead(s):
        return ((x + s[0]) % nx) * 2 + (c + s[1]) % 2

    def behind(s):
        return ((x + nx - s[0]) % nx) * 2 + (c + s[1]) % 2

    far = [(kx, kc) for kx in range(1, nx) for kc in range(2)]

    def part(q):
        return grad.at[:, pl.ds(pl.multiple_of(q * cols, 128), cols)]

    own_copy = copy(part(d), g.at[0, 0, z, 0])
    attn_copy = copy(attn, blocks.at[0, 0])
    mask_copy = copy(mask_hbm, mask)
    scale_copy = copy(scale_hbm, scale)
    w_copy = copy(w_hbm, w)
    barrier = pltpu.get_barrier_semaphore()

    def greet(dev):
        pl.semaphore_signal(barrier, inc=1, device_id=dev, device_id_type=MESH)

    for s in far + [(0, 1)]:
        greet(dp(ahead(s)))
    greet(beside)
    pl.when(z > 0)(lambda: greet(along(-1)))
    pl.when(z < na - 1)(lambda: greet(along(1)))
    pl.semaphore_wait(barrier, nd + (z + na - 1) // na + (2 * na - 2 - z) // na)

    both = RIGHT, LEFT = 0, 1

    def open_to(way):
        return z < na - 1 if way == RIGHT else z > 0

    def open_from(way):
        return z > 0 if way == RIGHT else z < na - 1

    def step(way):
        return 1 if way == RIGHT else -1

    def offer_z(k, kc):
        need_own(k, kc)
        src = g.at[0, k, z, kc] if k or kc else part(d)
        for way in both:
            send(("oz", k, kc, way), open_to(way), lambda: (src, g.at[0, k, z, kc]), along(step(way)))

    def offer_y(k, kc):
        need_own(k, kc)
        src = g.at[0, k, z, kc] if k or kc else part(d)
        send(("oy", k, kc), None, lambda: (src, g.at[1, k, z, kc]), beside)

    def need_own(k, kc):
        if k or kc:
            once(("swap", (k, kc)), None, lambda: g.at[0, k, z, kc], dp(behind((k, kc))))

    offer_z(0, 0)
    offer_y(0, 0)
    for s in far + [(0, 1)]:
        send(("swap", s), None, lambda s=s: (part(ahead(s)), g.at[0, s[0], z, s[1]]), dp(ahead(s)))
    for k in range(1, nx):
        send(("attn", k), None, lambda k=k: (attn, blocks.at[k, 0]), dp(ahead((k, 0))))
    send(("attn", 0), None, lambda: (attn, blocks.at[0, 1]), sibling)

    def unit(p, way):
        return z - p if way == RIGHT else z + p

    def held(p, way):
        return z >= p if way == RIGHT else z + p <= na - 1

    def due(p, way):
        return p > z if way == RIGHT else p > na - 1 - z

    def target(p, way):
        return na + z - p if way == RIGHT else z + p - na

    def ref_z(p, k, way, piece):
        u = unit(p, way)
        return g.at[0, k, u] if piece == 0 else g.at[1, k, u, :, :, rest]

    def ref_y(p, k, way, r):
        return g.at[r, k, unit(p, way), :, :, first]

    def need_z(p, k, piece):
        if p == 0 and piece:
            need_y(0, k)
        elif p == 0:
            if k == 0:
                copied(own_copy)
            need_own(k, 0)
            need_own(k, 1)
        for way in both if p else ():
            if p == 1 and piece == 0:
                for kc in range(2):
                    once(("oz", k, kc, way), held(p, way), lambda: g.at[0, k, unit(p, way), kc], along(-step(way)))
            else:
                once(("gz", p - 1, k, way, piece), held(p, way), lambda: ref_z(p, k, way, piece), along(-step(way)))

    def need_y(p, k):
        if p == 0:
            for kc in range(2):
                once(("oy", k, kc), None, lambda: g.at[1, k, z, kc], beside)
        for way in both if p else ():
            once(("gy", p, k, way), held(p, way), lambda: ref_y(p, k, way, 1), beside)

    def need_units(j):
        for p in range(j + 1):
            for k in range(nx):
                need_z(p, k, 0)
                need_y(p, k)
                need_z(p, k, 1)

    def tiles_of(span, fn):
        @pl.loop(0, span // TILE)
        def _(i):
            fn(pl.ds(pl.multiple_of(i * TILE, TILE), TILE))

    def gather_z(p, k, piece):
        need_z(p, k, piece)
        for way in both:
            def make(way=way):
                ref = ref_z(p, k, way, piece)
                return ref, ref
            send(("gz", p, k, way, piece), held(p, way) & open_to(way), make, along(step(way)))

    def gather_y(p, k):
        need_z(p, k, 0)
        for way in both:
            send(("gy", p, k, way), held(p, way),
                 lambda way=way: (ref_y(p, k, way, 0), ref_y(p, k, way, 1)), beside)

    def sum_y(p, k):
        for way in both[:1] if p == na else both:
            def make(way=way):
                t = target(p, way)
                return psy.at[k, t], ry.at[k, t]
            send(("sy", p, k, way), None if p == na else due(p, way), make, beside)

    def half(name, p, k):
        if (p, k) == (na - 1, 0) and name != "sb":
            return (1,) if name == "sa" else (0,)
        return ()

    def sum_z(name, p, k):
        rear = name == "sb"
        total, out, into, span = (pb, sb, rb, cols - cut) if rear else (pa, sa, ra, cut)
        before = "sb" if rear else "sa"
        sel = half(name, p, k)
        fresh = (before, p, k) not in seen
        seen.add((before, p, k))
        for way in both:
            def run(chained, way=way):
                t = target(p, way)
                if not rear and fresh:
                    arrive(("sy", p, k, way), ry.at[k, t], beside)
                if chained and fresh:
                    arrive((before, p - 1, k, way), into.at[way, k, t], along(-step(way)))

                def tile(at):
                    at = sel + (..., at)
                    val = total[(k, t) + at]
                    if not rear:
                        val += ry[(k, t) + at].astype(F32)
                    if chained:
                        val += into[(way, k, t) + at].astype(F32)
                    out[(k, t) + at] = val.astype(BF16)

                tiles_of(span, tile)

            now = due(p, way)
            pl.when(now & open_from(way))(lambda: run(True))
            pl.when(now & jnp.logical_not(open_from(way)))(lambda: run(False))

            def make(way=way):
                at = (k, target(p, way)) + sel
                return out.at[at], into.at[(way,) + at]
            send((name, p, k, way), now, make, along(step(way)))

    def add_last(name, k):
        total, into, span = (pb, rb, cols - cut) if name == "sb" else (pa, ra, cut)
        sel = half(name, na - 1, k)
        for way in both:
            def run(way=way):
                arrive((name, na - 1, k, way), into.at[(way, k, z) + sel], along(-step(way)))

                def tile(at):
                    at = sel + (..., at)
                    total[(k, z) + at] += into[(way, k, z) + at].astype(F32)
                tiles_of(span, tile)
            pl.when(open_from(way))(run)

    def put(kx, kc):
        val = (blocks[kx, kc].astype(F32) * gate[...]).astype(BF16).reshape(na, 2, rows, width)
        for bb in range(2):
            gated[(b + bb) % 2, kx, :, kc] = val[:, bb]

    def passed(k):
        arrive(("attn", k), blocks.at[k, 0], dp(behind((k, 0))))
        send(("pass", k), None, lambda: (blocks.at[k, 0], blocks.at[k, 1]), sibling)
        make_gate()
        put(k, 0)

    def make_gate():
        if "gate" in seen:
            return
        seen.add("gate")
        copied(mask_copy)
        copied(scale_copy)
        heads = scale.shape[0]
        each = width // heads
        for i in range(heads):
            gate[:, i * each:(i + 1) * each] = jnp.full((1, each), mask[i].astype(F32) * scale[i], F32)

    def take(k):
        make_gate()
        if k:
            arrive(("pass", k), blocks.at[k, 1], sibling)
        else:
            copied(attn_copy)
            put(0, 0)
            arrive(("attn", 0), blocks.at[0, 1], sibling)
        put(k, 1)

    def turn(k):
        span = na * 2 * rows
        for r in range(2):
            lo = (r * nx + k) * span
            gt[:, lo:lo + span] = gated[r, k].reshape(span, width).T

    def project(k):
        copied(w_copy)

        def dot(at):
            lhs = gated[:, k].reshape(2 * na * 2 * rows, width)
            res = jnp.dot(lhs, w[:, at], preferred_element_type=F32)
            return res.reshape(2, na, 2, rows, TILE)

        def front(at):
            res = dot(at)
            pa[k, :, :, :, at] = res[0]
            psy[k, :, :, :, at] = res[1].astype(BF16)

        @pl.loop(cut // TILE, cols // TILE)
        def _(i):
            res = dot(pl.ds(pl.multiple_of(i * TILE, TILE), TILE))
            low = pl.ds(pl.multiple_of(i * TILE - cut, TILE), TILE)
            for r in range(2):
                pb[k, :, r, :, :, low] = res[r]

        tiles_of(cut, front)

    small = jnp.minimum(z, na - 1 - z)

    def nth(j):
        if j == 0:
            return z
        near = z - (j + 1) // 2 if j % 2 else z + (j + 1) // 2
        end = jnp.where(z == small, j, na - 1 - j)
        return jnp.where(j <= 2 * small, near, end)

    def back(j):
        need_units(j)
        copied(w_copy)
        u = nth(j)

        def tile(at):
            lhs = g[:, :, u].reshape(2 * nx * 2 * rows, cols)
            res = lax.dot_general(lhs, w[at, :], (((1,), (1,)), ((), ())), preferred_element_type=F32)
            res = res.reshape(2, nx, 2, rows, TILE)
            bs[j, :, :, :, at] = res[:, :, 1].astype(BF16)
            bo[j, :, :, :, at] = res[:, :, 0]

        tiles_of(width, tile)
        send(("pair", j), None, lambda: (bs.at[j], br.at[j]), sibling)

    def cross(j):
        arrive(("pair", j), br.at[j], sibling)
        for k in range(1, nx):
            bs2[j, k - 1] = (bo[j, :, k] + br[j, :, k].astype(F32)).astype(BF16)
            send(("cross", j, k), None, lambda k=k: (bs2.at[j, k - 1], br2.at[j, k - 1]), dp(behind((k, 0))))

    def attn_out(j):
        for k in range(1, nx):
            arrive(("cross", j, k), br2.at[j, k - 1], dp(ahead((k, 0))))
        total = bo[j, :, 0] + br[j, :, 0].astype(F32)
        for k in range(1, nx):
            total += br2[j, k - 1].astype(F32)
        total = (total * gate[...].reshape(1, 1, width)).astype(BF16)
        for r in range(2):
            ga[nth(j), (b + r) % 2] = total[r]
        copy(ga.at[nth(j)], ga_out.at[nth(j)])

    def weight(i):
        need_units(na - 1)
        slot, each = len(tiles) % SLOTS, cols // nd
        if len(tiles) >= SLOTS:
            copied(tiles[-SLOTS])
        at = slice(i * TILE, (i + 1) * TILE)
        gw[slot] = jnp.dot(gt[...], g[:, :, :, :, :, at].reshape(tokens, TILE), preferred_element_type=F32)
        lo = i * TILE % each
        tiles.append(copy(gw.at[slot], gw_outs[i * TILE // each].at[:, lo:lo + TILE]))

    def last_b(k):
        add_last("sb", k)
        fb[k] = pb[k, z, 1].astype(BF16)
        send(("fy", k), None, lambda: (fb.at[k], ryf.at[k]), beside)

    def finish(k, which):
        once(("sy", na, k, RIGHT), None, lambda: ry.at[k, z], beside)

        def tile(at):
            for kc in which:
                fin[k, kc, :, at] = (pa[k, z, kc, :, at] + ry[k, z, kc, :, at].astype(F32)).astype(BF16)

        tiles_of(cut, tile)
        once(("fy", k), None, lambda: ryf.at[k], beside)
        for kc in which:
            fin[k, kc, :, cut:] = (pb[k, z, 0, kc] + ryf[k, kc].astype(F32)).astype(BF16)
            if (k, kc) != (0, 0):
                send(("home", (k, kc)), None, lambda kc=kc: (fin.at[k, kc], pj_out.at[d]), dp(behind((k, kc))))
            else:
                copy(fin.at[0, 0], pj_out.at[d])

    steps = {
        "oz": offer_z, "oy": offer_y, "gz": gather_z, "gy": gather_y, "sy": sum_y, "sa": functools.partial(sum_z, "sa"),
        "sb": functools.partial(sum_z, "sb"), "sc": functools.partial(sum_z, "sc"), "pass": passed, "put": take, "proj": project, "turn": turn,
        "back": back, "cross": cross, "ga": attn_out, "gw": weight, "fb": last_b,
        "fa": functools.partial(add_last, "sa"), "fc": functools.partial(add_last, "sc"),
        "fin": lambda k: finish(k, (0, 1) if k else (1,)), "fic": lambda k: finish(k, (0,)),
    }
    for name, *at in plan(na, nx, cols // TILE):
        steps[name](*at)
    assert len(ids) <= rsem.shape[0]
    for s in [(0, 1)] + far:
        arrive(("home", s), pj_out.at[ahead(s)], dp(ahead(s)))
    for key, cond, make, dev in sent:
        when(cond, lambda: remote(key, *make(), dev).wait_send())
    for i in range(len(local)):
        copied(i)


def hand_over(pj, ga, *refs):
    *gw, proj, gattn, gw_out, sems = refs
    cols = pj.shape[2]
    each = cols // len(gw)
    pairs = [(gw[i], gw_out.at[:, i * each:(i + 1) * each]) for i in range(len(gw))]
    pairs += [(pj.at[i], proj.at[:, i * cols:(i + 1) * cols]) for i in range(len(gw))]
    pairs.append((ga, gattn))
    copies = [pltpu.make_async_copy(src, dst, sems.at[i]) for i, (src, dst) in enumerate(pairs)]
    for copy in copies:
        copy.start()
    for copy in copies:
        copy.wait()


def fused(nh, nd, attn_out, head_mask, gate_scale, w_out, grad_out):
    na, nx = nh // 2, nd // 2
    rows, cols, width = grad_out.shape[0], w_out.shape[1], w_out.shape[0]
    tokens = rows * nh * nd
    cut = split(cols, SUM_SHARE, TILE)
    n_sems = semaphores(na, nx, cols // TILE)
    vmem = pl.BlockSpec(memory_space=pltpu.VMEM)
    hbm = pl.BlockSpec(memory_space=pltpu.HBM)
    free = pl.BlockSpec(memory_space=pl.ANY)
    order = (2, nx, na, 2, rows)
    half = (nx, na, 2, rows)
    whole = (nx, na, 2, 2, rows)
    pj, ga, *gw = pl.pallas_call(
        functools.partial(kernel, nh, nd),
        out_shape=(
            jax.ShapeDtypeStruct((nd, rows, cols), BF16),
            jax.ShapeDtypeStruct((na, 2, rows, width), BF16),
        ) + (jax.ShapeDtypeStruct((width, cols // nd), F32),) * nd,
        in_specs=[hbm] * 5,
        out_specs=(free,) * (2 + nd),
        scratch_shapes=[
            pltpu.SMEM(head_mask.shape, head_mask.dtype),
            pltpu.SMEM(gate_scale.shape, F32),
            pltpu.VMEM((1, width), F32),
            pltpu.VMEM((nx, 2, nh * rows, width), BF16),
            pltpu.VMEM(order + (width,), BF16),
            pltpu.VMEM((width, tokens), BF16),
            pltpu.VMEM(w_out.shape, BF16),
            pltpu.VMEM(order + (cols,), BF16),
            pltpu.VMEM(half + (cut,), F32),
            pltpu.VMEM(whole + (cols - cut,), F32),
            pltpu.VMEM(half + (cut,), BF16),
            pltpu.VMEM(half + (cut,), BF16),
            pltpu.VMEM(half + (cut,), BF16),
            pltpu.VMEM(whole + (cols - cut,), BF16),
            pltpu.VMEM((2,) + half + (cut,), BF16),
            pltpu.VMEM((2,) + whole + (cols - cut,), BF16),
            pltpu.VMEM((nx, 2, rows, cols - cut), BF16),
            pltpu.VMEM((nx, 2, rows, cols - cut), BF16),
            pltpu.VMEM((nx, 2, rows, cols), BF16),
            pltpu.VMEM((na, 2, nx, rows, width), BF16),
            pltpu.VMEM((na, 2, nx, rows, width), F32),
            pltpu.VMEM((na, 2, nx, rows, width), BF16),
            pltpu.VMEM((na, nx - 1, 2, rows, width), BF16),
            pltpu.VMEM((na, nx - 1, 2, rows, width), BF16),
            pltpu.VMEM((na, 2, rows, width), BF16),
            pltpu.VMEM((SLOTS, width, TILE), F32),
            pltpu.SemaphoreType.DMA((1,)),
            pltpu.SemaphoreType.DMA((n_sems,)),
            pltpu.SemaphoreType.DMA((6 + na + cols // TILE,)),
        ],
        compiler_params=pltpu.CompilerParams(
            collective_id=0, has_side_effects=True, vmem_limit_bytes=VMEM_LIMIT
        ),
    )(*[pltpu.with_memory_space_constraint(a, pltpu.HBM) for a in (attn_out, head_mask, gate_scale, grad_out, w_out)])
    proj, gattn, gw = pl.pallas_call(
        hand_over,
        out_shape=(
            jax.ShapeDtypeStruct(grad_out.shape, BF16),
            jax.ShapeDtypeStruct(attn_out.shape, BF16),
            jax.ShapeDtypeStruct(w_out.shape, F32),
        ),
        in_specs=[vmem] * (2 + nd),
        out_specs=(hbm,) * 3,
        scratch_shapes=[pltpu.SemaphoreType.DMA((2 * nd + 1,))],
        compiler_params=pltpu.CompilerParams(vmem_limit_bytes=HAND_LIMIT),
    )(pj, ga.reshape(attn_out.shape), *gw)
    return proj, gattn, gw


def shards(attn_out, head_mask, gate_scale, w_out, grad_out):
    n_dp, n_head = lax.axis_size("dp"), lax.axis_size("head")
    rows, (width, cols) = grad_out.shape[0], w_out.shape
    if rows % 16 == 0 and n_dp % 2 == 0 and n_head % 2 == 0 and min(n_dp, n_head) > 2 and width % TILE == 0 and cols % (2 * TILE) == 0 and cols % (n_dp * 128) == 0 and (width // head_mask.shape[0]) % 128 == 0:
        return fused(n_head, n_dp, attn_out, head_mask, gate_scale, w_out, grad_out)
    gate_vals = head_mask.astype(jnp.float32) * gate_scale
    width_each = attn_out.shape[1] // gate_vals.shape[0]
    col_gate = jnp.repeat(gate_vals, width_each)
    gated = (attn_out.astype(jnp.float32) * col_gate[None, :]).astype(jnp.bfloat16)
    mine = lax.all_to_all(grad_out, "dp", 1, 0, tiled=True)
    every = lax.all_gather(mine.reshape(n_dp, rows, cols), "head", axis=1)
    grad_cols = every.reshape(n_dp * n_head * rows, cols)
    gated_all = lax.all_gather(gated, "dp", axis=0, tiled=True)
    part = jnp.dot(gated_all, w_out, preferred_element_type=jnp.float32).astype(jnp.bfloat16)
    summed = lax.psum_scatter(part.reshape(n_dp, n_head, rows, cols), "head", scatter_dimension=1, tiled=False)
    proj_out = lax.all_to_all(summed.reshape(n_dp * rows, cols), "dp", 0, 1, tiled=True)
    back = lax.dot_general(grad_cols, w_out, (((1,), (1,)), ((), ())), preferred_element_type=jnp.float32)
    back = lax.psum_scatter(back.astype(jnp.bfloat16), "dp", scatter_dimension=0, tiled=True)
    grad_attn = (back.astype(jnp.float32) * col_gate[None, :]).astype(jnp.bfloat16)
    grad_w = lax.dot_general(gated_all, grad_cols, (((0,), (0,)), ((), ())), preferred_element_type=jnp.float32)
    return (proj_out, grad_attn, grad_w)


def solution(mesh):
    return jax.shard_map(
        shards,
        mesh=mesh,
        in_specs=(P("dp", "head"), P("head"), P("head"), P("head", "dp"), P(("dp", "head"), None)),
        out_specs=(P(("dp", "head"), None), P("dp", "head"), P("head", "dp")),
        check_vma=False,
    )
```

```python
import functools

import jax
import jax.numpy as jnp
from jax import lax
from jax.experimental import pallas as pl
from jax.experimental.pallas import tpu as pltpu
from jax.sharding import PartitionSpec as P

MESH = pl.DeviceIdType.MESH
F32, BF16 = jnp.float32, jnp.bfloat16
TILE = 256
SUM_SHARE = 5, 8
GATHER_SHARE = 9, 16
VMEM_LIMIT = 41 * 1024 * 1024
HAND_LIMIT = 2 * 1024 * 1024
SLOTS = 3


ORDER = (
    ("oy", 0, 1), ("oz", 0, 1), ("put", 0), ("oy", 1, 0), ("turn", 0), ("oz", 1, 0), ("oy", 1, 1),
    ("oz", 1, 1), ("gz", 0, 0, 1), ("proj", 0), ("gz", 1, 0, 0), ("sy", 1, 0), ("sy", 2, 0), ("gz", 0, 1, 1),
    ("gz", 1, 1, 0), ("gy", 1, 0), ("back", 0), ("sb", 1, 0), ("gy", 1, 1), ("pass", 1), ("sa", 1, 0),
    ("sb", 2, 0), ("put", 1), ("gz", 2, 0, 0), ("gz", 1, 0, 1), ("proj", 1), ("gz", 1, 1, 1), ("sy", 1, 1),
    ("sy", 2, 1), ("gy", 2, 0), ("sb", 1, 1), ("cross", 0), ("gz", 2, 1, 0), ("gy", 2, 1), ("turn", 1),
    ("sa", 1, 1), ("sb", 2, 1), ("sy", 3, 1), ("sa", 2, 1), ("gy", 3, 0), ("gz", 2, 0, 1), ("sa", 2, 0),
    ("gz", 2, 1, 1), ("back", 2), ("sb", 3, 1), ("gy", 3, 1), ("sy", 3, 0), ("cross", 2), ("back", 1),
    ("ga", 0), ("sy", 4, 1), ("cross", 1), ("sa", 3, 1), ("back", 3), ("gw", 7), ("sb", 3, 0), ("cross", 3),
    ("fb", 1), ("gw", 3), ("gw", 5), ("sy", 4, 0), ("gw", 6), ("fa", 1), ("gw", 2), ("fin", 1), ("sa", 3, 0),
    ("gw", 0), ("fb", 0), ("sc", 3, 0), ("ga", 1), ("gw", 1), ("ga", 2), ("fa", 0), ("gw", 4), ("fin", 0),
    ("fc", 0), ("ga", 3), ("fic", 0),
)


def split(cols, share, tile):
    tiles = cols // tile
    return max(1, min(tiles - 1, tiles * share[0] // share[1])) * tile


def plan(na, nx, tiles):
    order = [("oz", 0, 1), ("oy", 0, 1), ("put", 0), ("proj", 0)]
    for k in range(1, nx):
        order += [(name, k, kc) for kc in range(2) for name in ("oz", "oy")]
    order += [("gz", 0, 0, 1), ("sy", 1, 0), ("turn", 0)]
    for k in range(1, nx):
        order += [("gz", 0, k, 1), ("pass", k)]
    for k in range(1, nx):
        order += [("put", k), ("proj", k), ("sy", 1, k), ("turn", k)]
    for p in range(1, na):
        for k in range(nx):
            order += [("gz", p, k, 0)] if p < na - 1 else []
            order += [("gy", p, k), ("sb", p, k)]
            order += [("gz", p, k, 1)] if p < na - 1 else []
            order += [("sa", p, k), ("sy", p + 1, k)]
        order += [("sc", p, 0)] if p == na - 1 else []
        order += [("cross", p - 2)] if p > 1 else []
        order += [("back", p - 1)]
    order += [("cross", na - 2), ("back", na - 1)]
    order += [("fb", k) for k in range(nx)] + [("fa", k) for k in range(nx)] + [("cross", na - 1)]
    order += [("fin", k) for k in reversed(range(nx))] + [("fc", 0), ("fic", 0)]
    order += [("gw", i) for i in range(tiles)] + [("ga", j) for j in range(na)]
    return ORDER if set(ORDER) == set(order) else order


def semaphores(na, nx, tiles):
    each = {"oz": 2, "oy": 1, "sy": 2, "sa": 2, "sb": 2, "sc": 2, "pass": 1, "back": 1, "cross": nx - 1, "fb": 1, "fin": 2}
    return 3 + 2 * nx + nx + 2 * nx + sum(each.get(step[0], 0) for step in plan(na, nx, tiles))


def kernel(nh, nd, attn, mask_hbm, scale_hbm, grad, w_hbm, pj_out, ga_out, *more):
    gw_outs, more = more[:nd], more[nd:]
    (mask, scale, gate, blocks, gated, gt, w, g, pa, pb, psy, ry, sa, sb, ra, rb, fb, ryf, fin,
     bs, bo, br, bs2, br2, ga, gw, ssem, rsem, lsem) = more
    na, nx = nh // 2, nd // 2
    h, d = lax.axis_index("head"), lax.axis_index("dp")
    z, b = h // 2, h % 2
    x, c = d // 2, d % 2
    rows, cols = g.shape[-2:]
    width, tokens = gt.shape
    cut, mid = split(cols, SUM_SHARE, TILE), split(cols, GATHER_SHARE, 128)
    first, rest = pl.ds(0, mid), pl.ds(mid, cols - mid)
    sent, ids, seen = [], {}, set()
    local, tiles = [], []

    def when(cond, fn):
        if cond is None:
            fn()
        else:
            pl.when(cond)(fn)

    def remote(key, src, dst, dev):
        if key[0] in ("gz", "sa", "sb"):
            key = ("z", *key[1:4], key[4] if key[0] == "gz" else int(key[0] == "sb"))
        if key[0] in ("gy", "sy"):
            key = ("y", *key[1:])
        i = ids.setdefault(key, len(ids))
        return pltpu.make_async_remote_copy(
            src_ref=src, dst_ref=dst, send_sem=ssem.at[0], recv_sem=rsem.at[i],
            device_id=dev, device_id_type=MESH,
        )

    def send(key, cond, make, dev):
        when(cond, lambda: remote(key, *make(), dev).start())
        sent.append((key, cond, make, dev))

    def arrive(key, ref, dev):
        remote(key, ref, ref, dev).wait_recv()

    def once(key, cond, make, dev):
        if key not in seen:
            seen.add(key)
            when(cond, lambda: arrive(key, make(), dev))

    def copy(src, dst):
        made = pltpu.make_async_copy(src, dst, lsem.at[len(local)])
        made.start()
        local.append(made)
        return len(local) - 1

    def copied(i):
        if local[i] is not None:
            local[i].wait()
            local[i] = None

    def dp(q):
        return {"head": h, "dp": q}

    def along(step):
        return {"head": (h + 2 * step + nh) % nh, "dp": d}

    beside = {"head": z * 2 + 1 - b, "dp": d}
    sibling = dp(x * 2 + 1 - c)

    def ahead(s):
        return ((x + s[0]) % nx) * 2 + (c + s[1]) % 2

    def behind(s):
        return ((x + nx - s[0]) % nx) * 2 + (c + s[1]) % 2

    far = [(kx, kc) for kx in range(1, nx) for kc in range(2)]

    def part(q):
        return grad.at[:, pl.ds(pl.multiple_of(q * cols, 128), cols)]

    own_copy = copy(part(d), g.at[0, 0, z, 0])
    attn_copy = copy(attn, blocks.at[0, 0])
    mask_copy = copy(mask_hbm, mask)
    scale_copy = copy(scale_hbm, scale)
    w_copy = copy(w_hbm, w)
    barrier = pltpu.get_barrier_semaphore()

    def greet(dev):
        pl.semaphore_signal(barrier, inc=1, device_id=dev, device_id_type=MESH)

    for s in far + [(0, 1)]:
        greet(dp(ahead(s)))
    greet(beside)
    pl.when(z > 0)(lambda: greet(along(-1)))
    pl.when(z < na - 1)(lambda: greet(along(1)))
    pl.semaphore_wait(barrier, nd + (z + na - 1) // na + (2 * na - 2 - z) // na)

    both = RIGHT, LEFT = 0, 1

    def open_to(way):
        return z < na - 1 if way == RIGHT else z > 0

    def open_from(way):
        return z > 0 if way == RIGHT else z < na - 1

    def step(way):
        return 1 if way == RIGHT else -1

    def offer_z(k, kc):
        need_own(k, kc)
        if (k, kc) == (0, 0):
            copied(own_copy)
        src = g.at[0, k, z, kc]
        for way in both:
            send(("oz", k, kc, way), open_to(way), lambda: (src, g.at[0, k, z, kc]), along(step(way)))

    def offer_y(k, kc):
        need_own(k, kc)
        if (k, kc) == (0, 0):
            copied(own_copy)
        src = g.at[0, k, z, kc]
        send(("oy", k, kc), None, lambda: (src, g.at[1, k, z, kc]), beside)

    def need_own(k, kc):
        if k or kc:
            once(("swap", (k, kc)), None, lambda: g.at[0, k, z, kc], dp(behind((k, kc))))

    offer_z(0, 0)
    offer_y(0, 0)
    for s in far + [(0, 1)]:
        send(("swap", s), None, lambda s=s: (part(ahead(s)), g.at[0, s[0], z, s[1]]), dp(ahead(s)))
    for k in range(1, nx):
        send(("attn", k), None, lambda k=k: (attn, blocks.at[k, 0]), dp(ahead((k, 0))))
    send(("attn", 0), None, lambda: (attn, blocks.at[0, 1]), sibling)

    def unit(p, way):
        return z - p if way == RIGHT else z + p

    def held(p, way):
        return z >= p if way == RIGHT else z + p <= na - 1

    def due(p, way):
        return p > z if way == RIGHT else p > na - 1 - z

    def target(p, way):
        return na + z - p if way == RIGHT else z + p - na

    def ref_z(p, k, way, piece):
        u = unit(p, way)
        return g.at[0, k, u] if piece == 0 else g.at[1, k, u, :, :, rest]

    def ref_y(p, k, way, r):
        return g.at[r, k, unit(p, way), :, :, first]

    def need_z(p, k, piece):
        if p == 0 and piece:
            need_y(0, k)
        elif p == 0:
            if k == 0:
                copied(own_copy)
            need_own(k, 0)
            need_own(k, 1)
        for way in both if p else ():
            if p == 1 and piece == 0:
                for kc in range(2):
                    once(("oz", k, kc, way), held(p, way), lambda: g.at[0, k, unit(p, way), kc], along(-step(way)))
            else:
                once(("gz", p - 1, k, way, piece), held(p, way), lambda: ref_z(p, k, way, piece), along(-step(way)))

    def need_y(p, k):
        if p == 0:
            for kc in range(2):
                once(("oy", k, kc), None, lambda: g.at[1, k, z, kc], beside)
        for way in both if p else ():
            once(("gy", p, k, way), held(p, way), lambda: ref_y(p, k, way, 1), beside)

    def need_units(j):
        for p in range(j + 1):
            for k in range(nx):
                need_z(p, k, 0)
                need_y(p, k)
                need_z(p, k, 1)

    def tiles_of(span, fn):
        @pl.loop(0, span // TILE)
        def _(i):
            fn(pl.ds(pl.multiple_of(i * TILE, TILE), TILE))

    def gather_z(p, k, piece):
        need_z(p, k, piece)
        for way in both:
            def make(way=way):
                ref = ref_z(p, k, way, piece)
                return ref, ref
            send(("gz", p, k, way, piece), held(p, way) & open_to(way), make, along(step(way)))

    def gather_y(p, k):
        need_z(p, k, 0)
        for way in both:
            send(("gy", p, k, way), held(p, way),
                 lambda way=way: (ref_y(p, k, way, 0), ref_y(p, k, way, 1)), beside)

    def sum_y(p, k):
        for way in both[:1] if p == na else both:
            def make(way=way):
                t = target(p, way)
                return psy.at[k, t], ry.at[k, t]
            send(("sy", p, k, way), None if p == na else due(p, way), make, beside)

    def half(name, p, k):
        if (p, k) == (na - 1, 0) and name != "sb":
            return (1,) if name == "sa" else (0,)
        return ()

    def sum_z(name, p, k):
        rear = name == "sb"
        total, out, into, span = (pb, sb, rb, cols - cut) if rear else (pa, sa, ra, cut)
        before = "sb" if rear else "sa"
        sel = half(name, p, k)
        fresh = (before, p, k) not in seen
        seen.add((before, p, k))
        for way in both:
            def run(chained, way=way):
                t = target(p, way)
                if not rear and fresh:
                    arrive(("sy", p, k, way), ry.at[k, t], beside)
                if chained and fresh:
                    arrive((before, p - 1, k, way), into.at[way, k, t], along(-step(way)))

                def tile(at):
                    at = sel + (..., at)
                    val = total[(k, t) + at]
                    if not rear:
                        val += ry[(k, t) + at].astype(F32)
                    if chained:
                        val += into[(way, k, t) + at].astype(F32)
                    out[(k, t) + at] = val.astype(BF16)

                tiles_of(span, tile)

            now = due(p, way)
            pl.when(now & open_from(way))(lambda: run(True))
            pl.when(now & jnp.logical_not(open_from(way)))(lambda: run(False))

            def make(way=way):
                at = (k, target(p, way)) + sel
                return out.at[at], into.at[(way,) + at]
            send((name, p, k, way), now, make, along(step(way)))

    def add_last(name, k):
        total, into, span = (pb, rb, cols - cut) if name == "sb" else (pa, ra, cut)
        sel = half(name, na - 1, k)
        for way in both:
            def run(way=way):
                arrive((name, na - 1, k, way), into.at[(way, k, z) + sel], along(-step(way)))

                def tile(at):
                    at = sel + (..., at)
                    total[(k, z) + at] += into[(way, k, z) + at].astype(F32)
                tiles_of(span, tile)
            pl.when(open_from(way))(run)

    def put(kx, kc):
        val = (blocks[kx, kc].astype(F32) * gate[...]).astype(BF16).reshape(na, 2, rows, width)
        for bb in range(2):
            gated[(b + bb) % 2, kx, :, kc] = val[:, bb]

    def passed(k):
        arrive(("attn", k), blocks.at[k, 0], dp(behind((k, 0))))
        send(("pass", k), None, lambda: (blocks.at[k, 0], blocks.at[k, 1]), sibling)
        make_gate()
        put(k, 0)

    def make_gate():
        if "gate" in seen:
            return
        seen.add("gate")
        copied(mask_copy)
        copied(scale_copy)
        heads = scale.shape[0]
        each = width // heads
        for i in range(heads):
            gate[:, i * each:(i + 1) * each] = jnp.full((1, each), mask[i].astype(F32) * scale[i], F32)

    def take(k):
        make_gate()
        if k:
            arrive(("pass", k), blocks.at[k, 1], sibling)
        else:
            copied(attn_copy)
            put(0, 0)
            arrive(("attn", 0), blocks.at[0, 1], sibling)
        put(k, 1)

    def turn(k):
        span = na * 2 * rows
        for r in range(2):
            lo = (r * nx + k) * span
            gt[:, lo:lo + span] = gated[r, k].reshape(span, width).T

    def project(k):
        copied(w_copy)

        def dot(at):
            lhs = gated[:, k].reshape(2 * na * 2 * rows, width)
            res = jnp.dot(lhs, w[:, at], preferred_element_type=F32)
            return res.reshape(2, na, 2, rows, TILE)

        def front(at):
            res = dot(at)
            pa[k, :, :, :, at] = res[0]
            psy[k, :, :, :, at] = res[1].astype(BF16)

        @pl.loop(cut // TILE, cols // TILE)
        def _(i):
            res = dot(pl.ds(pl.multiple_of(i * TILE, TILE), TILE))
            low = pl.ds(pl.multiple_of(i * TILE - cut, TILE), TILE)
            for r in range(2):
                pb[k, :, r, :, :, low] = res[r]

        tiles_of(cut, front)

    small = jnp.minimum(z, na - 1 - z)

    def nth(j):
        if j == 0:
            return z
        near = z - (j + 1) // 2 if j % 2 else z + (j + 1) // 2
        end = jnp.where(z == small, j, na - 1 - j)
        return jnp.where(j <= 2 * small, near, end)

    def back(j):
        need_units(j)
        copied(w_copy)
        u = nth(j)

        def tile(at):
            lhs = g[:, :, u].reshape(2 * nx * 2 * rows, cols)
            res = lax.dot_general(lhs, w[at, :], (((1,), (1,)), ((), ())), preferred_element_type=F32)
            res = res.reshape(2, nx, 2, rows, TILE)
            bs[j, :, :, :, at] = res[:, :, 1].astype(BF16)
            bo[j, :, :, :, at] = res[:, :, 0]

        tiles_of(width, tile)
        send(("pair", j), None, lambda: (bs.at[j], br.at[j]), sibling)

    def cross(j):
        arrive(("pair", j), br.at[j], sibling)
        for k in range(1, nx):
            bs2[j, k - 1] = (bo[j, :, k] + br[j, :, k].astype(F32)).astype(BF16)
            send(("cross", j, k), None, lambda k=k: (bs2.at[j, k - 1], br2.at[j, k - 1]), dp(behind((k, 0))))

    def attn_out(j):
        for k in range(1, nx):
            arrive(("cross", j, k), br2.at[j, k - 1], dp(ahead((k, 0))))
        total = bo[j, :, 0] + br[j, :, 0].astype(F32)
        for k in range(1, nx):
            total += br2[j, k - 1].astype(F32)
        total = (total * gate[...].reshape(1, 1, width)).astype(BF16)
        for r in range(2):
            ga[nth(j), (b + r) % 2] = total[r]
        copy(ga.at[nth(j)], ga_out.at[nth(j)])

    def weight(i):
        need_units(na - 1)
        slot, each = len(tiles) % SLOTS, cols // nd
        if len(tiles) >= SLOTS:
            copied(tiles[-SLOTS])
        at = slice(i * TILE, (i + 1) * TILE)
        gw[slot] = jnp.dot(gt[...], g[:, :, :, :, :, at].reshape(tokens, TILE), preferred_element_type=F32)
        lo = i * TILE % each
        tiles.append(copy(gw.at[slot], gw_outs[i * TILE // each].at[:, lo:lo + TILE]))

    def last_b(k):
        add_last("sb", k)
        fb[k] = pb[k, z, 1].astype(BF16)
        send(("fy", k), None, lambda: (fb.at[k], ryf.at[k]), beside)

    def finish(k, which):
        once(("sy", na, k, RIGHT), None, lambda: ry.at[k, z], beside)

        def tile(at):
            for kc in which:
                fin[k, kc, :, at] = (pa[k, z, kc, :, at] + ry[k, z, kc, :, at].astype(F32)).astype(BF16)

        tiles_of(cut, tile)
        once(("fy", k), None, lambda: ryf.at[k], beside)
        for kc in which:
            fin[k, kc, :, cut:] = (pb[k, z, 0, kc] + ryf[k, kc].astype(F32)).astype(BF16)
            if (k, kc) != (0, 0):
                send(("home", (k, kc)), None, lambda kc=kc: (fin.at[k, kc], pj_out.at[d]), dp(behind((k, kc))))
            else:
                copy(fin.at[0, 0], pj_out.at[d])

    steps = {
        "oz": offer_z, "oy": offer_y, "gz": gather_z, "gy": gather_y, "sy": sum_y, "sa": functools.partial(sum_z, "sa"),
        "sb": functools.partial(sum_z, "sb"), "sc": functools.partial(sum_z, "sc"), "pass": passed, "put": take, "proj": project, "turn": turn,
        "back": back, "cross": cross, "ga": attn_out, "gw": weight, "fb": last_b,
        "fa": functools.partial(add_last, "sa"), "fc": functools.partial(add_last, "sc"),
        "fin": lambda k: finish(k, (0, 1) if k else (1,)), "fic": lambda k: finish(k, (0,)),
    }
    for name, *at in plan(na, nx, cols // TILE):
        steps[name](*at)
    assert len(ids) <= rsem.shape[0]
    for s in [(0, 1)] + far:
        arrive(("home", s), pj_out.at[ahead(s)], dp(ahead(s)))
    for key, cond, make, dev in sent:
        when(cond, lambda: remote(key, *make(), dev).wait_send())
    for i in range(len(local)):
        copied(i)


def hand_over(pj, ga, *refs):
    *gw, proj, gattn, gw_out, sems = refs
    cols = pj.shape[2]
    each = cols // len(gw)
    pairs = [(gw[i], gw_out.at[:, i * each:(i + 1) * each]) for i in range(len(gw))]
    pairs += [(pj.at[i], proj.at[:, i * cols:(i + 1) * cols]) for i in range(len(gw))]
    pairs.append((ga, gattn))
    copies = [pltpu.make_async_copy(src, dst, sems.at[i]) for i, (src, dst) in enumerate(pairs)]
    for copy in copies:
        copy.start()
    for copy in copies:
        copy.wait()


def fused(nh, nd, attn_out, head_mask, gate_scale, w_out, grad_out):
    na, nx = nh // 2, nd // 2
    rows, cols, width = grad_out.shape[0], w_out.shape[1], w_out.shape[0]
    tokens = rows * nh * nd
    cut = split(cols, SUM_SHARE, TILE)
    n_sems = semaphores(na, nx, cols // TILE)
    vmem = pl.BlockSpec(memory_space=pltpu.VMEM)
    hbm = pl.BlockSpec(memory_space=pltpu.HBM)
    free = pl.BlockSpec(memory_space=pl.ANY)
    order = (2, nx, na, 2, rows)
    half = (nx, na, 2, rows)
    whole = (nx, na, 2, 2, rows)
    pj, ga, *gw = pl.pallas_call(
        functools.partial(kernel, nh, nd),
        out_shape=(
            jax.ShapeDtypeStruct((nd, rows, cols), BF16),
            jax.ShapeDtypeStruct((na, 2, rows, width), BF16),
        ) + (jax.ShapeDtypeStruct((width, cols // nd), F32),) * nd,
        in_specs=[hbm] * 5,
        out_specs=(free,) * (2 + nd),
        scratch_shapes=[
            pltpu.SMEM(head_mask.shape, head_mask.dtype),
            pltpu.SMEM(gate_scale.shape, F32),
            pltpu.VMEM((1, width), F32),
            pltpu.VMEM((nx, 2, nh * rows, width), BF16),
            pltpu.VMEM(order + (width,), BF16),
            pltpu.VMEM((width, tokens), BF16),
            pltpu.VMEM(w_out.shape, BF16),
            pltpu.VMEM(order + (cols,), BF16),
            pltpu.VMEM(half + (cut,), F32),
            pltpu.VMEM(whole + (cols - cut,), F32),
            pltpu.VMEM(half + (cut,), BF16),
            pltpu.VMEM(half + (cut,), BF16),
            pltpu.VMEM(half + (cut,), BF16),
            pltpu.VMEM(whole + (cols - cut,), BF16),
            pltpu.VMEM((2,) + half + (cut,), BF16),
            pltpu.VMEM((2,) + whole + (cols - cut,), BF16),
            pltpu.VMEM((nx, 2, rows, cols - cut), BF16),
            pltpu.VMEM((nx, 2, rows, cols - cut), BF16),
            pltpu.VMEM((nx, 2, rows, cols), BF16),
            pltpu.VMEM((na, 2, nx, rows, width), BF16),
            pltpu.VMEM((na, 2, nx, rows, width), F32),
            pltpu.VMEM((na, 2, nx, rows, width), BF16),
            pltpu.VMEM((na, nx - 1, 2, rows, width), BF16),
            pltpu.VMEM((na, nx - 1, 2, rows, width), BF16),
            pltpu.VMEM((na, 2, rows, width), BF16),
            pltpu.VMEM((SLOTS, width, TILE), F32),
            pltpu.SemaphoreType.DMA((1,)),
            pltpu.SemaphoreType.DMA((n_sems,)),
            pltpu.SemaphoreType.DMA((6 + na + cols // TILE,)),
        ],
        compiler_params=pltpu.CompilerParams(
            collective_id=0, has_side_effects=True, vmem_limit_bytes=VMEM_LIMIT
        ),
    )(*[pltpu.with_memory_space_constraint(a, pltpu.HBM) for a in (attn_out, head_mask, gate_scale, grad_out, w_out)])
    proj, gattn, gw = pl.pallas_call(
        hand_over,
        out_shape=(
            jax.ShapeDtypeStruct(grad_out.shape, BF16),
            jax.ShapeDtypeStruct(attn_out.shape, BF16),
            jax.ShapeDtypeStruct(w_out.shape, F32),
        ),
        in_specs=[vmem] * (2 + nd),
        out_specs=(hbm,) * 3,
        scratch_shapes=[pltpu.SemaphoreType.DMA((2 * nd + 1,))],
        compiler_params=pltpu.CompilerParams(vmem_limit_bytes=HAND_LIMIT),
    )(pj, ga.reshape(attn_out.shape), *gw)
    return proj, gattn, gw


def shards(attn_out, head_mask, gate_scale, w_out, grad_out):
    n_dp, n_head = lax.axis_size("dp"), lax.axis_size("head")
    rows, (width, cols) = grad_out.shape[0], w_out.shape
    if rows % 16 == 0 and n_dp % 2 == 0 and n_head % 2 == 0 and min(n_dp, n_head) > 2 and width % TILE == 0 and cols % (2 * TILE) == 0 and cols % (n_dp * 128) == 0 and (width // head_mask.shape[0]) % 128 == 0:
        return fused(n_head, n_dp, attn_out, head_mask, gate_scale, w_out, grad_out)
    gate_vals = head_mask.astype(jnp.float32) * gate_scale
    width_each = attn_out.shape[1] // gate_vals.shape[0]
    col_gate = jnp.repeat(gate_vals, width_each)
    gated = (attn_out.astype(jnp.float32) * col_gate[None, :]).astype(jnp.bfloat16)
    mine = lax.all_to_all(grad_out, "dp", 1, 0, tiled=True)
    every = lax.all_gather(mine.reshape(n_dp, rows, cols), "head", axis=1)
    grad_cols = every.reshape(n_dp * n_head * rows, cols)
    gated_all = lax.all_gather(gated, "dp", axis=0, tiled=True)
    part = jnp.dot(gated_all, w_out, preferred_element_type=jnp.float32).astype(jnp.bfloat16)
    summed = lax.psum_scatter(part.reshape(n_dp, n_head, rows, cols), "head", scatter_dimension=1, tiled=False)
    proj_out = lax.all_to_all(summed.reshape(n_dp * rows, cols), "dp", 0, 1, tiled=True)
    back = lax.dot_general(grad_cols, w_out, (((1,), (1,)), ((), ())), preferred_element_type=jnp.float32)
    back = lax.psum_scatter(back.astype(jnp.bfloat16), "dp", scatter_dimension=0, tiled=True)
    grad_attn = (back.astype(jnp.float32) * col_gate[None, :]).astype(jnp.bfloat16)
    grad_w = lax.dot_general(gated_all, grad_cols, (((0,), (0,)), ((), ())), preferred_element_type=jnp.float32)
    return (proj_out, grad_attn, grad_w)


def solution(mesh):
    return jax.shard_map(
        shards,
        mesh=mesh,
        in_specs=(P("dp", "head"), P("head"), P("head"), P("head", "dp"), P(("dp", "head"), None)),
        out_specs=(P(("dp", "head"), None), P("dp", "head"), P("head", "dp")),
        check_vma=False,
    )
```

```python
import functools

import jax
import jax.numpy as jnp
from jax import lax
from jax.experimental import pallas as pl
from jax.experimental.pallas import tpu as pltpu
from jax.sharding import PartitionSpec as P

MESH = pl.DeviceIdType.MESH
F32, BF16 = jnp.float32, jnp.bfloat16
TILE = 256
SUM_SHARE = 5, 8
GATHER_SHARE = 9, 16
VMEM_LIMIT = 41 * 1024 * 1024
HAND_LIMIT = 2 * 1024 * 1024
SLOTS = 3


ORDER = (
    ("oy", 0, 1), ("oz", 0, 1), ("put", 0), ("oy", 1, 0), ("turn", 0), ("oz", 1, 0), ("oy", 1, 1),
    ("oz", 1, 1), ("gz", 0, 0, 1), ("proj", 0), ("gz", 1, 0, 0), ("sy", 1, 0), ("sy", 2, 0), ("gz", 0, 1, 1),
    ("gz", 1, 1, 0), ("gy", 1, 0), ("back", 0), ("sb", 1, 0), ("gy", 1, 1), ("pass", 1), ("sa", 1, 0),
    ("sb", 2, 0), ("put", 1), ("gz", 2, 0, 0), ("gz", 1, 0, 1), ("proj", 1), ("gz", 1, 1, 1), ("sy", 1, 1),
    ("sy", 2, 1), ("gy", 2, 0), ("sb", 1, 1), ("cross", 0), ("gz", 2, 1, 0), ("gy", 2, 1), ("turn", 1),
    ("sa", 1, 1), ("sb", 2, 1), ("sy", 3, 1), ("sa", 2, 1), ("gy", 3, 0), ("gz", 2, 0, 1), ("sa", 2, 0),
    ("gz", 2, 1, 1), ("back", 2), ("sb", 3, 1), ("gy", 3, 1), ("sy", 3, 0), ("cross", 2), ("back", 1),
    ("ga", 0), ("sy", 4, 1), ("cross", 1), ("sa", 3, 1), ("back", 3), ("gw", 7), ("sb", 3, 0), ("cross", 3),
    ("fb", 1), ("gw", 3), ("gw", 5), ("sy", 4, 0), ("gw", 6), ("fa", 1), ("gw", 2), ("fin", 1), ("sa", 3, 0),
    ("gw", 0), ("fb", 0), ("sc", 3, 0), ("ga", 1), ("gw", 1), ("ga", 2), ("fa", 0), ("gw", 4), ("fin", 0),
    ("fc", 0), ("ga", 3), ("fic", 0),
)


def split(cols, share, tile):
    tiles = cols // tile
    return max(1, min(tiles - 1, tiles * share[0] // share[1])) * tile


def plan(na, nx, tiles):
    order = [("oz", 0, 1), ("oy", 0, 1), ("put", 0), ("proj", 0)]
    for k in range(1, nx):
        order += [(name, k, kc) for kc in range(2) for name in ("oz", "oy")]
    order += [("gz", 0, 0, 1), ("sy", 1, 0), ("turn", 0)]
    for k in range(1, nx):
        order += [("gz", 0, k, 1), ("pass", k)]
    for k in range(1, nx):
        order += [("put", k), ("proj", k), ("sy", 1, k), ("turn", k)]
    for p in range(1, na):
        for k in range(nx):
            order += [("gz", p, k, 0)] if p < na - 1 else []
            order += [("gy", p, k), ("sb", p, k)]
            order += [("gz", p, k, 1)] if p < na - 1 else []
            order += [("sa", p, k), ("sy", p + 1, k)]
        order += [("sc", p, 0)] if p == na - 1 else []
        order += [("cross", p - 2)] if p > 1 else []
        order += [("back", p - 1)]
    order += [("cross", na - 2), ("back", na - 1)]
    order += [("fb", k) for k in range(nx)] + [("fa", k) for k in range(nx)] + [("cross", na - 1)]
    order += [("fin", k) for k in reversed(range(nx))] + [("fc", 0), ("fic", 0)]
    order += [("gw", i) for i in range(tiles)] + [("ga", j) for j in range(na)]
    return ORDER if set(ORDER) == set(order) else order


def semaphores(na, nx, tiles):
    each = {"sy": 2, "sa": 2, "sb": 2, "sc": 2, "pass": 1, "back": 1, "cross": nx - 1, "fb": 1, "fin": 2}
    return 8 * nx + sum(each.get(step[0], 0) for step in plan(na, nx, tiles))


def kernel(nh, nd, attn, mask_hbm, scale_hbm, grad, w_hbm, pj_out, ga_out, *more):
    gw_outs, more = more[:nd], more[nd:]
    (mask, scale, gate, blocks, gated, gt, w, g, pa, pb, psy, ry, sa, sb, ra, rb, fb, ryf, fin,
     bs, bo, br, bs2, br2, ga, gw, ssem, rsem, lsem) = more
    na, nx = nh // 2, nd // 2
    h, d = lax.axis_index("head"), lax.axis_index("dp")
    z, b = h // 2, h % 2
    x, c = d // 2, d % 2
    rows, cols = g.shape[-2:]
    width, tokens = gt.shape
    cut, mid = split(cols, SUM_SHARE, TILE), split(cols, GATHER_SHARE, 128)
    first, rest = pl.ds(0, mid), pl.ds(mid, cols - mid)
    sent, ids, seen = [], {}, set()
    local, tiles = [], []

    def when(cond, fn):
        if cond is None:
            fn()
        else:
            pl.when(cond)(fn)

    def remote(key, src, dst, dev):
        if key[0] in ("gz", "sa", "sb"):
            key = ("z", *key[1:4], key[4] if key[0] == "gz" else int(key[0] == "sb"))
        if key[0] in ("gy", "sy"):
            key = ("y", *key[1:])
        if key[0] in ("oz", "oy"):
            key = (*key[:2], *key[3:])
        i = ids.setdefault(key, len(ids))
        return pltpu.make_async_remote_copy(
            src_ref=src, dst_ref=dst, send_sem=ssem.at[0], recv_sem=rsem.at[i],
            device_id=dev, device_id_type=MESH,
        )

    def send(key, cond, make, dev):
        when(cond, lambda: remote(key, *make(), dev).start())
        sent.append((key, cond, make, dev))

    def arrive(key, ref, dev):
        remote(key, ref, ref, dev).wait_recv()

    def once(key, cond, make, dev):
        if key not in seen:
            seen.add(key)
            when(cond, lambda: arrive(key, make(), dev))

    def copy(src, dst, sem=None):
        made = pltpu.make_async_copy(src, dst, lsem.at[len(local) - len(tiles) + SLOTS if sem is None else sem])
        made.start()
        local.append(made)
        return len(local) - 1

    def copied(i):
        if local[i] is not None:
            local[i].wait()
            local[i] = None

    def dp(q):
        return {"head": h, "dp": q}

    def along(step):
        return {"head": (h + 2 * step + nh) % nh, "dp": d}

    beside = {"head": z * 2 + 1 - b, "dp": d}
    sibling = dp(x * 2 + 1 - c)

    def ahead(s):
        return ((x + s[0]) % nx) * 2 + (c + s[1]) % 2

    def behind(s):
        return ((x + nx - s[0]) % nx) * 2 + (c + s[1]) % 2

    far = [(kx, kc) for kx in range(1, nx) for kc in range(2)]

    def part(q):
        return grad.at[:, pl.ds(pl.multiple_of(q * cols, 128), cols)]

    own_copy = copy(part(d), g.at[0, 0, z, 0])
    attn_copy = copy(attn, blocks.at[0, 0])
    mask_copy = copy(mask_hbm, mask)
    scale_copy = copy(scale_hbm, scale)
    w_copy = copy(w_hbm, w)
    barrier = pltpu.get_barrier_semaphore()

    def greet(dev):
        pl.semaphore_signal(barrier, inc=1, device_id=dev, device_id_type=MESH)

    for s in far + [(0, 1)]:
        greet(dp(ahead(s)))
    greet(beside)
    pl.when(z > 0)(lambda: greet(along(-1)))
    pl.when(z < na - 1)(lambda: greet(along(1)))
    pl.semaphore_wait(barrier, nd + (z + na - 1) // na + (2 * na - 2 - z) // na)

    both = RIGHT, LEFT = 0, 1

    def open_to(way):
        return z < na - 1 if way == RIGHT else z > 0

    def open_from(way):
        return z > 0 if way == RIGHT else z < na - 1

    def step(way):
        return 1 if way == RIGHT else -1

    def offer_z(k, kc):
        need_own(k, kc)
        if (k, kc) == (0, 0):
            copied(own_copy)
        src = g.at[0, k, z, kc]
        for way in both:
            send(("oz", k, kc, way), open_to(way), lambda: (src, g.at[0, k, z, kc]), along(step(way)))

    def offer_y(k, kc):
        need_own(k, kc)
        if (k, kc) == (0, 0):
            copied(own_copy)
        src = g.at[0, k, z, kc]
        send(("oy", k, kc), None, lambda: (src, g.at[1, k, z, kc]), beside)

    def need_own(k, kc):
        if k or kc:
            once(("swap", (k, kc)), None, lambda: g.at[0, k, z, kc], dp(behind((k, kc))))

    offer_z(0, 0)
    offer_y(0, 0)
    for s in far + [(0, 1)]:
        send(("swap", s), None, lambda s=s: (part(ahead(s)), g.at[0, s[0], z, s[1]]), dp(ahead(s)))
    for k in range(1, nx):
        send(("attn", k), None, lambda k=k: (attn, blocks.at[k, 0]), dp(ahead((k, 0))))
    send(("attn", 0), None, lambda: (attn, blocks.at[0, 1]), sibling)

    def unit(p, way):
        return z - p if way == RIGHT else z + p

    def held(p, way):
        return z >= p if way == RIGHT else z + p <= na - 1

    def due(p, way):
        return p > z if way == RIGHT else p > na - 1 - z

    def target(p, way):
        return na + z - p if way == RIGHT else z + p - na

    def ref_z(p, k, way, piece):
        u = unit(p, way)
        return g.at[0, k, u] if piece == 0 else g.at[1, k, u, :, :, rest]

    def ref_y(p, k, way, r):
        return g.at[r, k, unit(p, way), :, :, first]

    def need_z(p, k, piece):
        if p == 0 and piece:
            need_y(0, k)
        elif p == 0:
            if k == 0:
                copied(own_copy)
            need_own(k, 0)
            need_own(k, 1)
        for way in both if p else ():
            if p == 1 and piece == 0:
                once(("oz", k, 0, way), held(p, way), lambda: g.at[0, k, unit(p, way)], along(-step(way)))
            else:
                once(("gz", p - 1, k, way, piece), held(p, way), lambda: ref_z(p, k, way, piece), along(-step(way)))

    def need_y(p, k):
        if p == 0:
            once(("oy", k, 0), None, lambda: g.at[1, k, z], beside)
        for way in both if p else ():
            once(("gy", p, k, way), held(p, way), lambda: ref_y(p, k, way, 1), beside)

    def need_units(j):
        for p in range(j + 1):
            for k in range(nx):
                need_z(p, k, 0)
                need_y(p, k)
                need_z(p, k, 1)

    def tiles_of(span, fn):
        @pl.loop(0, span // TILE)
        def _(i):
            fn(pl.ds(pl.multiple_of(i * TILE, TILE), TILE))

    def gather_z(p, k, piece):
        need_z(p, k, piece)
        for way in both:
            def make(way=way):
                ref = ref_z(p, k, way, piece)
                return ref, ref
            send(("gz", p, k, way, piece), held(p, way) & open_to(way), make, along(step(way)))

    def gather_y(p, k):
        need_z(p, k, 0)
        for way in both:
            send(("gy", p, k, way), held(p, way),
                 lambda way=way: (ref_y(p, k, way, 0), ref_y(p, k, way, 1)), beside)

    def sum_y(p, k):
        for way in both[:1] if p == na else both:
            def make(way=way):
                t = target(p, way)
                return psy.at[k, t], ry.at[k, t]
            send(("sy", p, k, way), None if p == na else due(p, way), make, beside)

    def half(name, p, k):
        if (p, k) == (na - 1, 0) and name != "sb":
            return (1,) if name == "sa" else (0,)
        return ()

    def sum_z(name, p, k):
        rear = name == "sb"
        total, out, into, span = (pb, sb, rb, cols - cut) if rear else (pa, sa, ra, cut)
        before = "sb" if rear else "sa"
        sel = half(name, p, k)
        fresh = (before, p, k) not in seen
        seen.add((before, p, k))
        for way in both:
            def run(chained, way=way):
                t = target(p, way)
                if not rear and fresh:
                    arrive(("sy", p, k, way), ry.at[k, t], beside)
                if chained and fresh:
                    arrive((before, p - 1, k, way), into.at[way, k, t], along(-step(way)))

                def tile(at):
                    at = sel + (..., at)
                    val = total[(k, t) + at]
                    if not rear:
                        val += ry[(k, t) + at].astype(F32)
                    if chained:
                        val += into[(way, k, t) + at].astype(F32)
                    out[(k, t) + at] = val.astype(BF16)

                tiles_of(span, tile)

            now = due(p, way)
            pl.when(now & open_from(way))(lambda: run(True))
            pl.when(now & jnp.logical_not(open_from(way)))(lambda: run(False))

            def make(way=way):
                at = (k, target(p, way)) + sel
                return out.at[at], into.at[(way,) + at]
            send((name, p, k, way), now, make, along(step(way)))

    def add_last(name, k):
        total, into, span = (pb, rb, cols - cut) if name == "sb" else (pa, ra, cut)
        sel = half(name, na - 1, k)
        for way in both:
            def run(way=way):
                arrive((name, na - 1, k, way), into.at[(way, k, z) + sel], along(-step(way)))

                def tile(at):
                    at = sel + (..., at)
                    total[(k, z) + at] += into[(way, k, z) + at].astype(F32)
                tiles_of(span, tile)
            pl.when(open_from(way))(run)

    def put(kx, kc):
        val = (blocks[kx, kc].astype(F32) * gate[...]).astype(BF16).reshape(na, 2, rows, width)
        for bb in range(2):
            gated[(b + bb) % 2, kx, :, kc] = val[:, bb]

    def passed(k):
        arrive(("attn", k), blocks.at[k, 0], dp(behind((k, 0))))
        send(("pass", k), None, lambda: (blocks.at[k, 0], blocks.at[k, 1]), sibling)
        make_gate()
        put(k, 0)

    def make_gate():
        if "gate" in seen:
            return
        seen.add("gate")
        copied(mask_copy)
        copied(scale_copy)
        heads = scale.shape[0]
        each = width // heads
        for i in range(heads):
            gate[:, i * each:(i + 1) * each] = jnp.full((1, each), mask[i].astype(F32) * scale[i], F32)

    def take(k):
        make_gate()
        if k:
            arrive(("pass", k), blocks.at[k, 1], sibling)
        else:
            copied(attn_copy)
            put(0, 0)
            arrive(("attn", 0), blocks.at[0, 1], sibling)
        put(k, 1)

    def turn(k):
        span = na * 2 * rows
        for r in range(2):
            lo = (r * nx + k) * span
            gt[:, lo:lo + span] = gated[r, k].reshape(span, width).T

    def project(k):
        copied(w_copy)

        def dot(at):
            lhs = gated[:, k].reshape(2 * na * 2 * rows, width)
            res = jnp.dot(lhs, w[:, at], preferred_element_type=F32)
            return res.reshape(2, na, 2, rows, TILE)

        def front(at):
            res = dot(at)
            pa[k, :, :, :, at] = res[0]
            psy[k, :, :, :, at] = res[1].astype(BF16)

        @pl.loop(cut // TILE, cols // TILE)
        def _(i):
            res = dot(pl.ds(pl.multiple_of(i * TILE, TILE), TILE))
            low = pl.ds(pl.multiple_of(i * TILE - cut, TILE), TILE)
            for r in range(2):
                pb[k, :, r, :, :, low] = res[r]

        tiles_of(cut, front)

    small = jnp.minimum(z, na - 1 - z)

    def nth(j):
        if j == 0:
            return z
        near = z - (j + 1) // 2 if j % 2 else z + (j + 1) // 2
        end = jnp.where(z == small, j, na - 1 - j)
        return jnp.where(j <= 2 * small, near, end)

    def back(j):
        need_units(j)
        copied(w_copy)
        u = nth(j)

        def tile(at):
            lhs = g[:, :, u].reshape(2 * nx * 2 * rows, cols)
            res = lax.dot_general(lhs, w[at, :], (((1,), (1,)), ((), ())), preferred_element_type=F32)
            res = res.reshape(2, nx, 2, rows, TILE)
            bs[j, :, :, :, at] = res[:, :, 1].astype(BF16)
            bo[j, :, :, :, at] = res[:, :, 0]

        tiles_of(width, tile)
        send(("pair", j), None, lambda: (bs.at[j], br.at[j]), sibling)

    def cross(j):
        arrive(("pair", j), br.at[j], sibling)
        for k in range(1, nx):
            bs2[j, k - 1] = (bo[j, :, k] + br[j, :, k].astype(F32)).astype(BF16)
            send(("cross", j, k), None, lambda k=k: (bs2.at[j, k - 1], br2.at[j, k - 1]), dp(behind((k, 0))))

    def attn_out(j):
        for k in range(1, nx):
            arrive(("cross", j, k), br2.at[j, k - 1], dp(ahead((k, 0))))
        total = bo[j, :, 0] + br[j, :, 0].astype(F32)
        for k in range(1, nx):
            total += br2[j, k - 1].astype(F32)
        total = (total * gate[...].reshape(1, 1, width)).astype(BF16)
        for r in range(2):
            ga[nth(j), (b + r) % 2] = total[r]
        copy(ga.at[nth(j)], ga_out.at[nth(j)])

    def weight(i):
        need_units(na - 1)
        slot, each = len(tiles) % SLOTS, cols // nd
        if len(tiles) >= SLOTS:
            copied(tiles[-SLOTS])
        at = slice(i * TILE, (i + 1) * TILE)
        gw[slot] = jnp.dot(gt[...], g[:, :, :, :, :, at].reshape(tokens, TILE), preferred_element_type=F32)
        lo = i * TILE % each
        tiles.append(copy(gw.at[slot], gw_outs[i * TILE // each].at[:, lo:lo + TILE], slot))

    def last_b(k):
        add_last("sb", k)
        fb[k] = pb[k, z, 1].astype(BF16)
        send(("fy", k), None, lambda: (fb.at[k], ryf.at[k]), beside)

    def finish(k, which):
        once(("sy", na, k, RIGHT), None, lambda: ry.at[k, z], beside)

        def tile(at):
            for kc in which:
                fin[k, kc, :, at] = (pa[k, z, kc, :, at] + ry[k, z, kc, :, at].astype(F32)).astype(BF16)

        tiles_of(cut, tile)
        once(("fy", k), None, lambda: ryf.at[k], beside)
        for kc in which:
            fin[k, kc, :, cut:] = (pb[k, z, 0, kc] + ryf[k, kc].astype(F32)).astype(BF16)
            if (k, kc) != (0, 0):
                send(("home", (k, kc)), None, lambda kc=kc: (fin.at[k, kc], pj_out.at[d]), dp(behind((k, kc))))
            else:
                copy(fin.at[0, 0], pj_out.at[d])

    steps = {
        "oz": offer_z, "oy": offer_y, "gz": gather_z, "gy": gather_y, "sy": sum_y, "sa": functools.partial(sum_z, "sa"),
        "sb": functools.partial(sum_z, "sb"), "sc": functools.partial(sum_z, "sc"), "pass": passed, "put": take, "proj": project, "turn": turn,
        "back": back, "cross": cross, "ga": attn_out, "gw": weight, "fb": last_b,
        "fa": functools.partial(add_last, "sa"), "fc": functools.partial(add_last, "sc"),
        "fin": lambda k: finish(k, (0, 1) if k else (1,)), "fic": lambda k: finish(k, (0,)),
    }
    for name, *at in plan(na, nx, cols // TILE):
        steps[name](*at)
    assert len(ids) <= rsem.shape[0]
    for s in [(0, 1)] + far:
        arrive(("home", s), pj_out.at[ahead(s)], dp(ahead(s)))
    for key, cond, make, dev in sent:
        when(cond, lambda: remote(key, *make(), dev).wait_send())
    for i in range(len(local)):
        copied(i)


def hand_over(pj, ga, *refs):
    *gw, proj, gattn, gw_out, sems = refs
    cols = pj.shape[2]
    each = cols // len(gw)
    pairs = [(gw[i], gw_out.at[:, i * each:(i + 1) * each]) for i in range(len(gw))]
    pairs += [(pj.at[i], proj.at[:, i * cols:(i + 1) * cols]) for i in range(len(gw))]
    pairs.append((ga, gattn))
    copies = [pltpu.make_async_copy(src, dst, sems.at[i]) for i, (src, dst) in enumerate(pairs)]
    for copy in copies:
        copy.start()
    for copy in copies:
        copy.wait()


def fused(nh, nd, attn_out, head_mask, gate_scale, w_out, grad_out):
    na, nx = nh // 2, nd // 2
    rows, cols, width = grad_out.shape[0], w_out.shape[1], w_out.shape[0]
    tokens = rows * nh * nd
    cut = split(cols, SUM_SHARE, TILE)
    n_sems = semaphores(na, nx, cols // TILE)
    vmem = pl.BlockSpec(memory_space=pltpu.VMEM)
    hbm = pl.BlockSpec(memory_space=pltpu.HBM)
    free = pl.BlockSpec(memory_space=pl.ANY)
    order = (2, nx, na, 2, rows)
    half = (nx, na, 2, rows)
    whole = (nx, na, 2, 2, rows)
    pj, ga, *gw = pl.pallas_call(
        functools.partial(kernel, nh, nd),
        out_shape=(
            jax.ShapeDtypeStruct((nd, rows, cols), BF16),
            jax.ShapeDtypeStruct((na, 2, rows, width), BF16),
        ) + (jax.ShapeDtypeStruct((width, cols // nd), F32),) * nd,
        in_specs=[hbm] * 5,
        out_specs=(free,) * (2 + nd),
        scratch_shapes=[
            pltpu.SMEM(head_mask.shape, head_mask.dtype),
            pltpu.SMEM(gate_scale.shape, F32),
            pltpu.VMEM((1, width), F32),
            pltpu.VMEM((nx, 2, nh * rows, width), BF16),
            pltpu.VMEM(order + (width,), BF16),
            pltpu.VMEM((width, tokens), BF16),
            pltpu.VMEM(w_out.shape, BF16),
            pltpu.VMEM(order + (cols,), BF16),
            pltpu.VMEM(half + (cut,), F32),
            pltpu.VMEM(whole + (cols - cut,), F32),
            pltpu.VMEM(half + (cut,), BF16),
            pltpu.VMEM(half + (cut,), BF16),
            pltpu.VMEM(half + (cut,), BF16),
            pltpu.VMEM(whole + (cols - cut,), BF16),
            pltpu.VMEM((2,) + half + (cut,), BF16),
            pltpu.VMEM((2,) + whole + (cols - cut,), BF16),
            pltpu.VMEM((nx, 2, rows, cols - cut), BF16),
            pltpu.VMEM((nx, 2, rows, cols - cut), BF16),
            pltpu.VMEM((nx, 2, rows, cols), BF16),
            pltpu.VMEM((na, 2, nx, rows, width), BF16),
            pltpu.VMEM((na, 2, nx, rows, width), F32),
            pltpu.VMEM((na, 2, nx, rows, width), BF16),
            pltpu.VMEM((na, nx - 1, 2, rows, width), BF16),
            pltpu.VMEM((na, nx - 1, 2, rows, width), BF16),
            pltpu.VMEM((na, 2, rows, width), BF16),
            pltpu.VMEM((SLOTS, width, TILE), F32),
            pltpu.SemaphoreType.DMA((1,)),
            pltpu.SemaphoreType.DMA((n_sems,)),
            pltpu.SemaphoreType.DMA((6 + na + SLOTS,)),
        ],
        compiler_params=pltpu.CompilerParams(
            collective_id=0, has_side_effects=True, vmem_limit_bytes=VMEM_LIMIT
        ),
    )(*[pltpu.with_memory_space_constraint(a, pltpu.HBM) for a in (attn_out, head_mask, gate_scale, grad_out, w_out)])
    proj, gattn, gw = pl.pallas_call(
        hand_over,
        out_shape=(
            jax.ShapeDtypeStruct(grad_out.shape, BF16),
            jax.ShapeDtypeStruct(attn_out.shape, BF16),
            jax.ShapeDtypeStruct(w_out.shape, F32),
        ),
        in_specs=[vmem] * (2 + nd),
        out_specs=(hbm,) * 3,
        scratch_shapes=[pltpu.SemaphoreType.DMA((2 * nd + 1,))],
        compiler_params=pltpu.CompilerParams(vmem_limit_bytes=HAND_LIMIT),
    )(pj, ga.reshape(attn_out.shape), *gw)
    return proj, gattn, gw


def shards(attn_out, head_mask, gate_scale, w_out, grad_out):
    n_dp, n_head = lax.axis_size("dp"), lax.axis_size("head")
    rows, (width, cols) = grad_out.shape[0], w_out.shape
    if rows % 16 == 0 and n_dp % 2 == 0 and n_head % 2 == 0 and min(n_dp, n_head) > 2 and width % TILE == 0 and cols % (2 * TILE) == 0 and cols % (n_dp * 128) == 0 and (width // head_mask.shape[0]) % 128 == 0:
        return fused(n_head, n_dp, attn_out, head_mask, gate_scale, w_out, grad_out)
    gate_vals = head_mask.astype(jnp.float32) * gate_scale
    width_each = attn_out.shape[1] // gate_vals.shape[0]
    col_gate = jnp.repeat(gate_vals, width_each)
    gated = (attn_out.astype(jnp.float32) * col_gate[None, :]).astype(jnp.bfloat16)
    mine = lax.all_to_all(grad_out, "dp", 1, 0, tiled=True)
    every = lax.all_gather(mine.reshape(n_dp, rows, cols), "head", axis=1)
    grad_cols = every.reshape(n_dp * n_head * rows, cols)
    gated_all = lax.all_gather(gated, "dp", axis=0, tiled=True)
    part = jnp.dot(gated_all, w_out, preferred_element_type=jnp.float32).astype(jnp.bfloat16)
    summed = lax.psum_scatter(part.reshape(n_dp, n_head, rows, cols), "head", scatter_dimension=1, tiled=False)
    proj_out = lax.all_to_all(summed.reshape(n_dp * rows, cols), "dp", 0, 1, tiled=True)
    back = lax.dot_general(grad_cols, w_out, (((1,), (1,)), ((), ())), preferred_element_type=jnp.float32)
    back = lax.psum_scatter(back.astype(jnp.bfloat16), "dp", scatter_dimension=0, tiled=True)
    grad_attn = (back.astype(jnp.float32) * col_gate[None, :]).astype(jnp.bfloat16)
    grad_w = lax.dot_general(gated_all, grad_cols, (((0,), (0,)), ((), ())), preferred_element_type=jnp.float32)
    return (proj_out, grad_attn, grad_w)


def solution(mesh):
    return jax.shard_map(
        shards,
        mesh=mesh,
        in_specs=(P("dp", "head"), P("head"), P("head"), P("head", "dp"), P(("dp", "head"), None)),
        out_specs=(P(("dp", "head"), None), P("dp", "head"), P("head", "dp")),
        check_vma=False,
    )
```
